32 devices in a mesh: energy: 8 (over y, x, core), section: 4 (over z).
Axes of the slice: x: 2, y: 2, z: 4, core: 2. Of those that a mesh axis runs over, the one named last changes fastest.
Arguments:
- self_in: float32 [32, 4, 2, 256, 256], P('energy', 'section'), as said below
- onsite: float32 [4, 256], P('section'), may hold values from -1 to 1
- within: float32 [4, 256, 256], P('section'), may hold values from -0.09375 to 0.09375
- between: float32 [4, 256, 256], P('section'), as said below
- coupling: float32 [4, 256, 256], P('section'), may hold values from -1 to 1
- groups: int32 [4, 256], P('section'), may hold values from 0 to 3
- offsets: int32 [3], replicated, may hold values from 1 to 2, as said below
- strength: float32 [3], replicated, may hold values from 0.3 to 1
Outputs:
- green: float32 [32, 4, 2, 256, 256], P('energy', 'section')
- self_out: float32 [32, 4, 2, 256, 256], P('energy', 'section')
The draws below stay inside these ranges and needn't reach their ends.
Inputs may be any that keep to these rules, and one draw needn't show every extreme that they name: `offsets`: every entry lies between 1 and 2, and one entry equals 2. `self_in`: imaginary parts of diagonal entries lie between -0.02 and -0.002, real parts of diagonal entries between -0.3 and 0.3; off-diagonal entries lie between -0.01 and 0.01. `between`: diagonal entries lie between 1.4 and 2.0; off-diagonal entries are at most 1.12 / sqrt(256) in magnitude.
All inputs are finite; a program needn't handle non-finite values.
Results may differ from the reference program's by a relative error of at most 0.0001.
Values sent between devices are 32-bit elements; how exact they have to be, the bound alone decides.
A program may use at most 128 MiB of HBM per device.

```python
import math
import jax
import jax.numpy as jnp
from jax import lax

B = 256
NEWTON = 3
MODES = 3
GROUPS = 4
OFF_MAX = 2
ENERGIES = 32
SLABS = 4


def draw_self_in(key, part):
    shape = (ENERGIES, SLABS, 2, B, B)
    first_key = jax.random.fold_in(key, 11)
    second_key = jax.random.fold_in(key, 12)
    third_key = jax.random.fold_in(key, 13)
    spread = jnp.clip(0.004 * jax.random.normal(first_key, shape, jnp.float32), -0.01, 0.01)
    real_diag = jax.random.uniform(second_key, (ENERGIES, SLABS, B), jnp.float32, -0.3, 0.3)
    imag_diag = jax.random.uniform(third_key, (ENERGIES, SLABS, B), jnp.float32, -0.02, -0.002)
    identity = jnp.eye(B, dtype=jnp.float32)
    diagonal = jnp.stack([real_diag, imag_diag], axis=2)[..., :, None] * identity
    return spread * (1.0 - identity) + diagonal


def draw_between(key, part):
    diag_key = jax.random.fold_in(key, 31)
    rest_key = jax.random.fold_in(key, 32)
    identity = jnp.eye(B, dtype=jnp.float32)
    diag_values = jax.random.uniform(diag_key, (SLABS, B), jnp.float32, 1.4, 2.0)
    scale = 0.28 * B ** (-0.5)
    rest = jnp.clip(scale * jax.random.normal(rest_key, (SLABS, B, B), jnp.float32), -4.0 * scale, 4.0 * scale)
    return rest * (1.0 - identity) + diag_values[:, :, None] * identity


def draw_offsets(key, part):
    values = jax.random.randint(jax.random.fold_in(key, 21), (MODES,), 1, OFF_MAX + 1)
    chosen = jax.random.randint(jax.random.fold_in(key, 22), (), 0, MODES)
    return jnp.where(jnp.arange(MODES) == chosen, OFF_MAX, values).astype(jnp.int32)


def touch_ends(values, stream_key, low, largest):
    extent = values.shape
    index_at = [jax.random.randint(jax.random.fold_in(stream_key, axis), (), 0, extent[axis]) for axis in range(len(extent))]
    values = values.at[tuple(index_at)].set(low)
    longest = extent.index(max(extent))
    index_at[longest] = (index_at[longest] + 1) % extent[longest]
    return values.at[tuple(index_at)].set(largest)


def shard_levels(key, shape, cuts, low, largest):
    loudness, own = 1.0, jax.random.fold_in(key, 6)
    for axis_at, parts in cuts:
        steps = jnp.exp(jax.random.uniform(jax.random.fold_in(own, axis_at), (parts,), jnp.float32, low / len(cuts), largest / len(cuts)))
        loudness = loudness * jnp.repeat(steps, shape[axis_at] // parts).reshape([-1 if axis == axis_at else 1 for axis in range(len(shape))])
    return loudness


def normal_values(key, shape, scale, reach, shards=(), kind=jnp.bfloat16):
    level = shard_levels(key, shape, shards, -0.22, 0.18) if shards else 1.0
    array = jax.random.normal(key, shape, jnp.float32) * scale * level
    return jnp.minimum(jnp.maximum(array, -reach), reach).astype(kind)


def setup_inputs(seed: int = 0) -> dict:
    arg_keys = jax.random.split(jax.random.key(seed), 9)
    self_in = draw_self_in(jax.random.fold_in(arg_keys[8], 71), 0)
    onsite = jnp.clip(jax.random.uniform(arg_keys[1], (SLABS, B), jnp.float32, -1.0, 1.0) * shard_levels(arg_keys[1], (SLABS, B), ((0, 4),), -0.4, 0.0), -1.0, 1.0)
    within = normal_values(arg_keys[2], (SLABS, B, B), (16 * B) ** -0.5, 0.09375, ((0, 4),), jnp.float32)
    between = draw_between(jax.random.fold_in(arg_keys[8], 71), 0)
    coupling = normal_values(arg_keys[4], (SLABS, B, B), 0.18, 1.0, ((0, 4),), jnp.float32)
    groups = touch_ends(jax.random.randint(arg_keys[5], (SLABS, B), 0, GROUPS), jax.random.fold_in(arg_keys[5], 1), 0, GROUPS - 1).astype(jnp.int32)
    offsets = draw_offsets(jax.random.fold_in(arg_keys[8], 71), 0)
    strength = jnp.clip(jnp.exp(jax.random.uniform(arg_keys[7], (MODES,), jnp.float32, math.log(0.3), math.log(1.0))), 0.3, 1.0)
    return {"self_in": self_in, "onsite": onsite, "within": within, "between": between, "coupling": coupling, "groups": groups, "offsets": offsets, "strength": strength}


HIGH = lax.Precision.HIGHEST
ETA = 1.0
CONTACT = 0.6


def multiply(left, right):
    return jnp.einsum("...ij,...jk->...ik", left, right, precision=HIGH)


def product(left, right):
    real_a, imag_a = left[..., 0, :, :], left[..., 1, :, :]
    real_b, imag_b = right[..., 0, :, :], right[..., 1, :, :]
    return jnp.stack([multiply(real_a, real_b) - multiply(imag_a, imag_b),
                      multiply(real_a, imag_b) + multiply(imag_a, real_b)], axis=-3)


def times_real(field, matrix):
    return jnp.einsum("...ij,jk->...ik", field, matrix, precision=HIGH)


def real_times(matrix, field):
    return jnp.einsum("ij,...jk->...ik", matrix, field, precision=HIGH)


def newton(system):
    sys_re, sys_im = system[..., 0, :, :], system[..., 1, :, :]
    real_c = jnp.diagonal(sys_re, axis1=-2, axis2=-1)
    imag_c = jnp.diagonal(sys_im, axis1=-2, axis2=-1)
    modulus = real_c * real_c + imag_c * imag_c
    inv_re = real_c / modulus
    inv_im = -imag_c / modulus
    half_re = inv_re[..., :, None] * sys_re - inv_im[..., :, None] * sys_im
    half_im = inv_re[..., :, None] * sys_im + inv_im[..., :, None] * sys_re
    full_re = half_re * inv_re[..., None, :] - half_im * inv_im[..., None, :]
    full_im = half_re * inv_im[..., None, :] + half_im * inv_re[..., None, :]
    identity = jnp.eye(system.shape[-1], dtype=jnp.float32)
    iterate = jnp.stack([2.0 * inv_re[..., :, None] * identity - full_re,
                         2.0 * inv_im[..., :, None] * identity - full_im], axis=-3)
    for sweep in range(NEWTON - 1):
        iterate = 2.0 * iterate - product(iterate, product(system, iterate))
    return iterate


def local_inverse(energy, hamil, sigma, previous, hop):
    identity = jnp.eye(hamil.shape[-1], dtype=jnp.float32)
    left = real_times(hop.T, times_real(previous, hop))
    sys_re = energy[..., None, None] * identity - hamil - sigma[..., 0, :, :] - left[..., 0, :, :]
    sys_im = ETA * identity - sigma[..., 1, :, :] - left[..., 1, :, :]
    return newton(jnp.stack([sys_re, sys_im], axis=-3))


def refine(local_green, incoming):
    return local_green + product(local_green, product(incoming, local_green))


def sandwich(hop, green):
    return times_real(real_times(hop, green), hop.T)


def reference(self_in, onsite, within, between, coupling, groups, offsets, strength):
    width = onsite.shape[1]
    identity = jnp.eye(width, dtype=jnp.float32)
    hams = onsite[:, :, None] * identity + 0.5 * (within + jnp.swapaxes(within, 1, 2))
    energies = -1.0 + (2 * jnp.arange(ENERGIES, dtype=jnp.int32) + 1).astype(jnp.float32) / ENERGIES
    contact = jnp.stack([jnp.zeros((width, width), jnp.float32), -CONTACT * identity])

    def one_energy(inputs):
        energy, sigma_all = inputs

        def forward(previous, items):
            hamil, hop, sigma = items
            local_green = local_inverse(energy, hamil, sigma, previous, hop)
            return local_green, local_green

        _, locals_all = lax.scan(forward, contact, (hams, between, sigma_all))

        def backward(incoming, items):
            local_green, hop = items
            full = refine(local_green, incoming)
            return sandwich(hop, full), full

        _, greens = lax.scan(backward, jnp.zeros((2, width, width), jnp.float32),
                             (locals_all, between), reverse=True)
        return greens

    green = lax.map(one_energy, (energies, self_in))
    padded = jnp.pad(green, ((OFF_MAX, OFF_MAX), (0, 0), (0, 0), (0, 0), (0, 0)))
    summed = jnp.zeros_like(green)
    for mode in range(MODES):
        shift = offsets[mode].astype(jnp.int32)
        lower = lax.dynamic_slice_in_dim(padded, (OFF_MAX - shift).astype(jnp.int32), ENERGIES, 0)
        upper = lax.dynamic_slice_in_dim(padded, (OFF_MAX + shift).astype(jnp.int32), ENERGIES, 0)
        summed = summed + strength[mode] * (lower + upper)
    mats = jnp.where(groups[:, :, None] == groups[:, None, :], coupling, jnp.float32(0.0))
    first = jnp.einsum("sab,eszbc->eszac", mats, summed, precision=HIGH)
    self_out = jnp.einsum("eszac,sdc->eszad", first, mats, precision=HIGH)
    return green, self_out
```

```python
import jax
import jax.numpy as jnp
from jax import lax
from jax.experimental import pallas as pl
from jax.experimental.pallas import tpu as pltpu
from jax.sharding import PartitionSpec as P

ETA = 1.0
CONTACT = 0.6
REACH = 2
CHUNKS = 4
PIECES = 2

F32 = jnp.float32
BF16 = jnp.bfloat16
MESH = pl.DeviceIdType.MESH


def split(value):
    high = value.astype(BF16)
    return high, (value - high.astype(F32)).astype(BF16)


def join(pieces, axis):
    return tuple(jnp.concatenate(parts, axis=axis) for parts in zip(*pieces))


def dot(left, right):
    return jnp.dot(left, right, preferred_element_type=F32)


def matmul(left, right):
    (left_h, left_l), (right_h, right_l) = left, right
    return dot(left_h, right_h) + (dot(left_h, right_l) + dot(left_l, right_h))


def minus(pair):
    return tuple(-part for part in pair)


def complex_columns(block):
    return join([join([block[0], block[1]], 1), join([minus(block[1]), block[0]], 1)], 0)


def complex_rows(block):
    return join(block, 1)


def splits(real, imag):
    return split(real), split(imag)


def rows_of(pair, start, size):
    return tuple(part[start : start + size] for part in pair)


def kernel(
    offsets, strength, self_in, onsite, within, between, coupling, groups,
    green, self_out,
    hamil, hops, mats, left, sigma, local, came_f, came_b, sent_b, given, field_y, halo,
    load_s, send_f, recv_f, send_b, recv_b, send_h, recv_h, send_x, recv_x, send_g, recv_g,
    turns,
):
    count, width = self_in.shape[0], self_in.shape[3]
    sections, place = lax.axis_size("section"), lax.axis_index("section")
    spans, seat = lax.axis_size("energy"), lax.axis_index("energy")
    last = sections - 1
    fold = max(sections - 2, 0)
    has_prev, has_next = place > 0, place < last
    has_low, has_high = seat > 0, seat < spans - 1
    folding, leaf = place == fold, place == last
    chunk, piece = width // CHUNKS, width // PIECES
    core = lax.rem(seat, 2)
    odd = core == 1
    partner = {"energy": seat + 1 - 2 * core}
    paced = sections > 2
    pacing = (place == 0) if paced else (place < 0)

    def order(step):
        return jnp.where(odd, count - 1 - step, step)

    def load(index):
        return pltpu.make_async_copy(self_in.at[index, 0], sigma.at[0, index], load_s.at[index])

    for step in range(count):
        load(order(step)).start()

    barrier = pltpu.get_barrier_semaphore()
    for present, target in (
        (has_prev, {"section": place - 1}),
        (has_next, {"section": place + 1}),
        (has_low, {"energy": seat - 1}),
        (has_high, {"energy": seat + 1}),
    ):
        @pl.when(present)
        def _():
            pl.semaphore_signal(barrier, inc=1, device_id=target, device_id_type=MESH)

    eye = (
        lax.broadcasted_iota(jnp.int32, (width, width), 0)
        == lax.broadcasted_iota(jnp.int32, (width, width), 1)
    )
    hop = between[0]
    own = jnp.where(eye, onsite[0:1, :], 0.0) + 0.5 * (within[0] + within[0].T)
    hamil[0] = own
    given[0] = hop
    given[1] = own

    peers = sum(present.astype(jnp.int32) for present in (has_prev, has_next, has_low, has_high))
    pl.semaphore_wait(barrier, peers)

    def give(index):
        return pltpu.make_async_remote_copy(
            src_ref=sigma.at[0, index], dst_ref=sigma.at[1, index],
            send_sem=send_x.at[index], recv_sem=recv_x.at[index],
            device_id={"section": place - 1}, device_id_type=MESH,
        )

    def give_shared():
        return pltpu.make_async_remote_copy(
            src_ref=given.at[core], dst_ref=given.at[2 + core],
            send_sem=send_g.at[0], recv_sem=recv_g.at[0],
            device_id={"section": place - 1}, device_id_type=MESH,
        )

    def give_partner():
        return pltpu.make_async_remote_copy(
            src_ref=given.at[2 + core], dst_ref=given.at[2 + core],
            send_sem=send_g.at[1], recv_sem=recv_g.at[1],
            device_id=partner, device_id_type=MESH,
        )

    @pl.when(leaf & has_prev)
    def _():
        give_shared().start()
        for step in range(count):
            index = order(step)
            load(index).wait()
            give(index).start()

    def set_hops(which, value):
        hops[which, 0], hops[which, 1] = split(value)
        hops[which, 2], hops[which, 3] = split(value.T)

    set_hops(0, hop)
    row_group = jnp.broadcast_to(groups[0:1, :].astype(F32), (width, width))
    mat = jnp.where(row_group == row_group.T, coupling[0], 0.0)
    mats[0], mats[1] = split(mat)
    mats[2], mats[3] = split(mat.T)

    @pl.when(seat == 0)
    def _():
        halo[0:REACH] = jnp.zeros((REACH, 2, width, width), F32)

    @pl.when(seat == spans - 1)
    def _():
        halo[REACH : 2 * REACH] = jnp.zeros((REACH, 2, width, width), F32)

    @pl.when(place == 0)
    def _():
        left[0] = jnp.zeros((width, width), F32)
        left[1] = -CONTACT * matmul((hops[0, 2], hops[0, 3]), (hops[0, 0], hops[0, 1]))

    @pl.when(folding & has_next)
    def _():
        give_shared().wait_recv()
        give_partner().start()
        give_partner().wait_recv()
        set_hops(1, given[2])
        hamil[1] = given[3]

    def forward_copy(which, index, part):
        rows = pl.ds(part * chunk, chunk)
        return pltpu.make_async_remote_copy(
            src_ref=local.at[which, index, :, rows], dst_ref=came_f.at[index, :, rows],
            send_sem=send_f.at[index, part], recv_sem=recv_f.at[index, part],
            device_id={"section": place + 1}, device_id_type=MESH,
        )

    def backward_copy(index, part):
        rows = pl.ds(part * chunk, chunk)
        return pltpu.make_async_remote_copy(
            src_ref=sent_b.at[index, :, rows], dst_ref=came_b.at[index, :, rows],
            send_sem=send_b.at[index, part], recv_sem=recv_b.at[index, part],
            device_id={"section": place - 1}, device_id_type=MESH,
        )

    def halo_up(index):
        slot = index - (count - REACH)
        return pltpu.make_async_remote_copy(
            src_ref=field_y.at[index], dst_ref=halo.at[slot],
            send_sem=send_h.at[slot], recv_sem=recv_h.at[slot],
            device_id={"energy": seat + 1}, device_id_type=MESH,
        )

    def halo_down(index):
        slot = index + REACH
        return pltpu.make_async_remote_copy(
            src_ref=field_y.at[index], dst_ref=halo.at[slot],
            send_sem=send_h.at[slot], recv_sem=recv_h.at[slot],
            device_id={"energy": seat - 1}, device_id_type=MESH,
        )

    def closing(which, halves):
        result = matmul((hops[which, 2], hops[which, 3]), join(halves, 0))
        left[0], left[1] = result[:, :width], result[:, width:]

    def contact(index, which):
        @pl.when((which == 0) & has_prev)
        def _():
            halves = []
            for part in range(CHUNKS):
                forward_copy(0, index, part).wait_recv()
                rows = slice(part * chunk, (part + 1) * chunk)
                field = [split(came_f[index, side, rows]) for side in range(2)]
                half = matmul(join(field, 0), (hops[0, 0], hops[0, 1]))
                halves.append(join([split(half[:chunk]), split(half[chunk:])], 1))
            closing(0, halves)

        @pl.when(which == 1)
        def _():
            field = [split(local[0, index, side]) for side in range(2)]
            half = matmul(join(field, 0), (hops[1, 0], hops[1, 1]))
            closing(1, [join([split(half[:width]), split(half[width:])], 1)])

    def inverse(index, which, step):
        number = jnp.full((1, width), 2 * (seat * count + index) + 1, jnp.int32)
        energy = -1.0 + number.astype(F32) / (count * spans)
        sys_re = jnp.where(eye, energy, 0.0) - hamil[which] - sigma[which, index, 0] - left[0]
        sys_im = jnp.where(eye, ETA, 0.0) - sigma[which, index, 1] - left[1]
        diag_re = jnp.where(eye, sys_re, 0.0)
        diag_im = jnp.where(eye, sys_im, 0.0)
        inverses = []
        for axis in (1, 0):
            real_c = jnp.sum(diag_re, axis=axis, keepdims=True)
            imag_c = jnp.sum(diag_im, axis=axis, keepdims=True)
            modulus = real_c * real_c + imag_c * imag_c
            inverses.append((real_c / modulus, -imag_c / modulus))
        (col_re, col_im), (row_re, row_im) = inverses
        rest_re = jnp.where(eye, 0.0, sys_im * row_im - sys_re * row_re)
        rest_im = jnp.where(eye, 0.0, -(sys_re * row_im + sys_im * row_re))
        rest = complex_rows(splits(rest_re, rest_im))
        square = matmul(rest, complex_columns(splits(rest_re, rest_im)))
        square_re, square_im = square[:, :width], square[:, width:]
        square = splits(square_re, square_im)
        powers = matmul(join([rest, complex_rows(square)], 0), complex_columns(square))
        sum_re = jnp.where(eye, 1.0, 0.0) + rest_re + square_re + powers[:width, :width]
        sum_im = rest_im + square_im + powers[:width, width:]
        base_re = col_re * sum_re - col_im * sum_im
        base_im = col_re * sum_im + col_im * sum_re
        base = complex_rows(splits(base_re, base_im))
        columns = complex_columns(splits(powers[width:, :width], powers[width:, width:]))
        if paced:
            @pl.when(pacing & ((step > 0) | odd))
            def _():
                pl.semaphore_wait(turns, 1)

        for start in range(0, width, piece):
            rows = slice(start, start + piece)
            out = matmul(rows_of(base, start, piece), columns)
            local[which, index, 0, rows] = base_re[rows] + out[:, :width]
            local[which, index, 1, rows] = base_im[rows] + out[:, width:]

            @pl.when(has_next & ((place < fold) | (which == 1)))
            def _():
                for part in range(start // chunk, (start + piece) // chunk):
                    forward_copy(which, index, part).start()

        if paced:
            @pl.when(pacing & ((step < count - 1) | (core == 0)))
            def _():
                forward_copy(which, index, CHUNKS - 2).wait_send()
                pl.semaphore_signal(turns, inc=1, device_id=partner, device_id_type=MESH)

    def forward(step):
        index = order(step)
        load(index).wait()

        def slab(which, carry):
            @pl.when(which == 1)
            def _():
                give(index).wait_recv()

            contact(index, which)
            inverse(index, which, step)
            return carry

        slabs = jnp.where(folding & has_next, 2, 1)
        lax.fori_loop(0, slabs, slab, 0)

    def finish(index):
        field = join([split(green[index, 0, side]) for side in range(2)], 0)
        half = matmul(field, (mats[2], mats[3]))
        half = join([split(half[:width]), split(half[width:])], 1)
        result = matmul((mats[0], mats[1]), half)
        field_y[index, 0] = result[:, :width]
        field_y[index, 1] = result[:, width:]

        @pl.when(has_high & (index >= count - REACH))
        def _():
            halo_up(index).start()

        @pl.when(has_low & (index < REACH))
        def _():
            halo_down(index).start()

    def send_back(index, start, size, out_re, out_im):
        rows = slice(start, start + size)
        sent_b[index, 0, rows] = out_re
        sent_b[index, 1, rows] = out_im
        for part in range(start // chunk, (start + size) // chunk):
            backward_copy(index, part).start()

    def backward(index):
        @pl.when(has_prev)
        def _():
            base = [split(local[0, index, side]) for side in range(2)]
            lefts = matmul((hops[0, 0], hops[0, 1]), join(base, 1))
            rights = matmul(join(base, 0), (hops[0, 2], hops[0, 3]))
            lefts = splits(lefts[:, :width], lefts[:, width:])
            columns = complex_columns(splits(rights[:width], rights[width:]))
            whole = matmul(join(lefts, 0), (hops[0, 2], hops[0, 3]))
            lefts = complex_rows(lefts)
            mids = []
            for part in range(CHUNKS):
                backward_copy(index, part).wait_recv()
                rows = slice(part * chunk, (part + 1) * chunk)
                incoming = join([split(came_b[index, side, rows]) for side in range(2)], 1)
                mids.append(matmul(incoming, columns))
            mid = jnp.concatenate(mids, axis=0)
            columns = complex_columns(splits(mid[:, :width], mid[:, width:]))
            for start in range(0, width, piece):
                out = matmul(rows_of(lefts, start, piece), columns)
                stop = start + piece
                send_back(
                    index, start, piece,
                    whole[start:stop] + out[:, :width],
                    whole[width + start : width + stop] + out[:, width:],
                )

        base_re, base_im = local[0, index, 0], local[0, index, 1]
        base = splits(base_re, base_im)
        columns = complex_columns(base)
        mids = []
        for part in range(CHUNKS):
            @pl.when(jnp.logical_not(has_prev))
            def _():
                backward_copy(index, part).wait_recv()

            rows = slice(part * chunk, (part + 1) * chunk)
            incoming = join([split(came_b[index, side, rows]) for side in range(2)], 1)
            mids.append(matmul(incoming, columns))
        mid = jnp.concatenate(mids, axis=0)
        out = matmul(complex_rows(base), complex_columns(splits(mid[:, :width], mid[:, width:])))
        green[index, 0, 0] = base_re + out[:, :width]
        green[index, 0, 1] = base_im + out[:, width:]
        finish(index)

    def refold(index):
        far_end = [split(local[1, index, side]) for side in range(2)]
        half = matmul((hops[1, 0], hops[1, 1]), join(far_end, 1))
        half = join([split(half[:, :width]), split(half[:, width:])], 0)
        incoming = matmul(half, (hops[1, 2], hops[1, 3]))
        incoming = splits(incoming[:width], incoming[width:])
        base_re, base_im = local[0, index, 0], local[0, index, 1]
        base = splits(base_re, base_im)
        mid = matmul(complex_rows(incoming), complex_columns(base))
        out = matmul(complex_rows(base), complex_columns(splits(mid[:, :width], mid[:, width:])))
        out_re, out_im = base_re + out[:, :width], base_im + out[:, width:]
        green[index, 0, 0] = out_re
        green[index, 0, 1] = out_im

        @pl.when(has_prev)
        def _():
            full = join(splits(out_re, out_im), 1)
            for start in range(0, width, piece):
                rows = pl.ds(start, piece)
                half = matmul((hops[0, 0, rows], hops[0, 1, rows]), full)
                half = join([split(half[:, :width]), split(half[:, width:])], 0)
                out = matmul(half, (hops[0, 2], hops[0, 3]))
                send_back(index, start, piece, out[:piece], out[piece:])

        finish(index)

    def receive(index):
        for part in range(CHUNKS):
            forward_copy(0, index, part).wait_recv()
        green[index, 0] = came_f[index]
        finish(index)

    behind = 2 * (fold - place)

    def turn(step, carry):
        @pl.when((place <= fold) & (step < count))
        def _():
            forward(step)

        @pl.when((place < fold) & (step >= behind) & (step < behind + count))
        def _():
            backward(order(step - behind))

        @pl.when(folding & has_next & (step < count))
        def _():
            refold(order(step))

        @pl.when(leaf & has_prev & (step < count))
        def _():
            receive(order(step))

        return carry

    lax.fori_loop(0, count + 2 * fold, turn, 0)

    near = jnp.float32(0.0)
    far = jnp.float32(0.0)
    for mode in range(offsets.shape[0]):
        near = near + jnp.where(offsets[mode] == 1, strength[mode], 0.0)
        far = far + jnp.where(offsets[mode] == 2, strength[mode], 0.0)

    @pl.when(has_high)
    def _():
        for slot in range(REACH):
            halo_down(slot).wait_recv()

    @pl.when(has_low)
    def _():
        for slot in range(REACH):
            halo_up(count - REACH + slot).wait_recv()

    def block(index, side):
        if index < 0:
            return halo[index + REACH, side]
        if index >= count:
            return halo[index - count + REACH, side]
        return field_y[index, side]

    for index in range(count):
        for side in range(2):
            self_out[index, 0, side] = near * (
                block(index - 1, side) + block(index + 1, side)
            ) + far * (block(index - 2, side) + block(index + 2, side))

    @pl.when(has_next)
    def _():
        for step in range(count):
            for part in range(CHUNKS):
                if paced and part == CHUNKS - 2:
                    waited = pacing & ((step < count - 1) | (core == 0))

                    @pl.when(jnp.logical_not(waited))
                    def _():
                        forward_copy(0, order(step), part).wait_send()
                else:
                    forward_copy(0, order(step), part).wait_send()

    @pl.when(has_prev & (place < last))
    def _():
        for index in range(count):
            for part in range(CHUNKS):
                backward_copy(index, part).wait_send()

    @pl.when(leaf & has_prev)
    def _():
        give_shared().wait_send()
        for index in range(count):
            give(index).wait_send()

    @pl.when(folding & has_next)
    def _():
        give_partner().wait_send()

    @pl.when(has_high)
    def _():
        for slot in range(REACH):
            halo_up(count - REACH + slot).wait_send()

    @pl.when(has_low)
    def _():
        for slot in range(REACH):
            halo_down(slot).wait_send()


def per_device(self_in, onsite, within, between, coupling, groups, offsets, strength):
    count, width = self_in.shape[0], self_in.shape[3]
    smem = pl.BlockSpec(memory_space=pltpu.SMEM)
    vmem = pl.BlockSpec(memory_space=pltpu.VMEM)
    anywhere = pl.BlockSpec(memory_space=pl.ANY)
    shape = jax.ShapeDtypeStruct(self_in.shape, F32)
    dma = pltpu.SemaphoreType.DMA
    blocks = pltpu.VMEM((count, 2, width, width), F32)
    return pl.pallas_call(
        kernel,
        out_shape=(shape, shape),
        in_specs=[smem] * 2 + [anywhere] + [vmem] * 5,
        out_specs=(vmem, vmem),
        scratch_shapes=[
            pltpu.VMEM((2, width, width), F32),
            pltpu.VMEM((2, 4, width, width), BF16),
            pltpu.VMEM((4, width, width), BF16),
            pltpu.VMEM((2, width, width), F32),
            pltpu.VMEM((2, count, 2, width, width), F32),
            pltpu.VMEM((2, count, 2, width, width), F32),
            blocks, blocks, blocks,
            pltpu.VMEM((4, width, width), F32),
            blocks,
            pltpu.VMEM((2 * REACH, 2, width, width), F32),
            dma((count,)),
            dma((count, CHUNKS)), dma((count, CHUNKS)), dma((count, CHUNKS)), dma((count, CHUNKS)),
            dma((2 * REACH,)), dma((2 * REACH,)),
            dma((count,)), dma((count,)), dma((2,)), dma((2,)),
            pltpu.SemaphoreType.REGULAR,
        ],
        compiler_params=pltpu.CompilerParams(
            collective_id=0, has_side_effects=True, vmem_limit_bytes=60 * 2**20
        ),
    )(offsets, strength, self_in, onsite, within, between, coupling, groups)


def solution(mesh):
    placed = (
        P("energy", "section", None, None, None),
        P("section", None),
        P("section", None, None),
        P("section", None, None),
        P("section", None, None),
        P("section", None),
        P(),
        P(),
    )
    return jax.shard_map(
        per_device,
        mesh=mesh,
        in_specs=placed,
        out_specs=(
            P("energy", "section", None, None, None),
            P("energy", "section", None, None, None),
        ),
        check_vma=False,
    )
```

```python
import jax
import jax.numpy as jnp
from jax import lax
from jax.experimental import pallas as pl
from jax.experimental.pallas import tpu as pltpu
from jax.sharding import PartitionSpec as P

ETA = 1.0
CONTACT = 0.6
REACH = 2
CHUNKS = 2
CUT = 4

F32 = jnp.float32
BF16 = jnp.bfloat16
MESH = pl.DeviceIdType.MESH


def split(value):
    high = value.astype(BF16)
    return high, (value - high.astype(F32)).astype(BF16)


def join(pieces, axis):
    return tuple(jnp.concatenate(parts, axis=axis) for parts in zip(*pieces))


def dot(left, right):
    return jnp.dot(left, right, preferred_element_type=F32)


def matmul(left, right):
    (left_h, left_l), (right_h, right_l) = left, right
    return dot(left_h, right_h) + (dot(left_h, right_l) + dot(left_l, right_h))


def minus(pair):
    return tuple(-part for part in pair)


def complex_columns(block):
    return join([join([block[0], block[1]], 1), join([minus(block[1]), block[0]], 1)], 0)


def complex_rows(block):
    return join(block, 1)


def splits(real, imag):
    return split(real), split(imag)


def complex_matmul(left, right):
    first = matmul(split(left[0]), split(right[0]))
    second = matmul(split(left[1]), split(right[1]))
    third = matmul(split(left[0] + left[1]), split(right[0] + right[1]))
    return first - second, third - first - second


def kernel(
    offsets, strength, self_in, onsite_in, within_in, between_in, coupling_in, groups_in,
    green, self_out,
    onsite, within, between, coupling, groups, load_p,
    hamil, hops, mats, left, sigma, local, came_f, came_b, sent_b, given, field_y, halo,
    load_s, send_f, recv_f, send_b, recv_b, send_h, recv_h, send_x, recv_x, send_g, recv_g,
    turns,
):
    count, width = self_in.shape[0], self_in.shape[3]
    sections, place = lax.axis_size("section"), lax.axis_index("section")
    spans, seat = lax.axis_size("energy"), lax.axis_index("energy")
    last = sections - 1
    fold = max(sections - 2, 0)
    has_prev, has_next = place > 0, place < last
    has_low, has_high = seat > 0, seat < spans - 1
    folding, leaf = place == fold, place == last
    edges = (0, width - width // CUT, width)
    spans_of = tuple(zip(edges[:-1], edges[1:]))
    core = lax.rem(seat, 2)
    odd = core == 1
    partner = {"energy": seat + 1 - 2 * core}
    paced = sections > 2
    pacing = (place == 0) if paced else (place < 0)

    def order(step):
        return jnp.where(odd, count - 1 - step, step)

    def load(index):
        return pltpu.make_async_copy(self_in.at[index, 0], sigma.at[0, index], load_s.at[index])

    params = [
        pltpu.make_async_copy(source, target, load_p.at[number])
        for number, (source, target) in enumerate(
            (
                (between_in, between), (within_in, within), (onsite_in, onsite),
                (groups_in, groups), (coupling_in, coupling),
            )
        )
    ]
    for param in params[:3]:
        param.start()
    for step in range(count):
        load(order(step)).start()
    for param in params[3:]:
        param.start()

    barrier = pltpu.get_barrier_semaphore()
    for present, target in (
        (has_prev, {"section": place - 1}),
        (has_next, {"section": place + 1}),
        (has_low, {"energy": seat - 1}),
        (has_high, {"energy": seat + 1}),
    ):
        @pl.when(present)
        def _():
            pl.semaphore_signal(barrier, inc=1, device_id=target, device_id_type=MESH)

    eye = (
        lax.broadcasted_iota(jnp.int32, (width, width), 0)
        == lax.broadcasted_iota(jnp.int32, (width, width), 1)
    )
    for param in params[:3]:
        param.wait()
    hop = between[0]
    own = jnp.where(eye, onsite[0:1, :], 0.0) + 0.5 * (within[0] + within[0].T)
    hamil[0] = own
    given[0] = hop
    given[1] = own

    def give(index):
        return pltpu.make_async_remote_copy(
            src_ref=sigma.at[0, index], dst_ref=sigma.at[1, index],
            send_sem=send_x.at[index], recv_sem=recv_x.at[index],
            device_id={"section": place - 1}, device_id_type=MESH,
        )

    def give_shared():
        return pltpu.make_async_remote_copy(
            src_ref=given.at[core], dst_ref=given.at[2 + core],
            send_sem=send_g.at[0], recv_sem=recv_g.at[0],
            device_id={"section": place - 1}, device_id_type=MESH,
        )

    def give_partner():
        return pltpu.make_async_remote_copy(
            src_ref=given.at[2 + core], dst_ref=given.at[2 + core],
            send_sem=send_g.at[1], recv_sem=recv_g.at[1],
            device_id=partner, device_id_type=MESH,
        )

    def set_hops(which, value):
        hops[which, 0], hops[which, 1] = split(value)
        hops[which, 2], hops[which, 3] = split(value.T)

    set_hops(0, hop)

    @pl.when(seat == 0)
    def _():
        halo[0:REACH] = jnp.zeros((REACH, 2, width, width), F32)

    @pl.when(seat == spans - 1)
    def _():
        halo[REACH : 2 * REACH] = jnp.zeros((REACH, 2, width, width), F32)

    @pl.when(place == 0)
    def _():
        left[0] = jnp.zeros((width, width), F32)
        left[1] = -CONTACT * matmul((hops[0, 2], hops[0, 3]), (hops[0, 0], hops[0, 1]))

    def set_mats():
        for param in params[3:]:
            param.wait()
        row_group = jnp.broadcast_to(groups[0:1, :].astype(F32), (width, width))
        mat = jnp.where(row_group == row_group.T, coupling[0], 0.0)
        mats[0], mats[1] = split(mat)
        mats[2], mats[3] = split(mat.T)

    peers = sum(present.astype(jnp.int32) for present in (has_prev, has_next, has_low, has_high))
    pl.semaphore_wait(barrier, peers)

    @pl.when(leaf & has_prev)
    def _():
        give_shared().start()
        for step in range(count):
            index = order(step)
            load(index).wait()
            give(index).start()

    @pl.when(has_prev)
    def _():
        set_mats()

    @pl.when(folding & has_next)
    def _():
        give_shared().wait_recv()
        give_partner().start()
        give_partner().wait_recv()
        set_hops(1, given[2])
        hamil[1] = given[3]

    def forward_copy(which, index, part):
        rows = pl.ds(edges[part], edges[part + 1] - edges[part])
        return pltpu.make_async_remote_copy(
            src_ref=local.at[which, index, :, rows], dst_ref=came_f.at[index, :, rows],
            send_sem=send_f.at[index, part], recv_sem=recv_f.at[index, part],
            device_id={"section": place + 1}, device_id_type=MESH,
        )

    def backward_copy(index, part):
        rows = pl.ds(edges[part], edges[part + 1] - edges[part])
        return pltpu.make_async_remote_copy(
            src_ref=sent_b.at[index, :, rows], dst_ref=came_b.at[index, :, rows],
            send_sem=send_b.at[index, part], recv_sem=recv_b.at[index, part],
            device_id={"section": place - 1}, device_id_type=MESH,
        )

    def halo_up(index):
        slot = index - (count - REACH)
        return pltpu.make_async_remote_copy(
            src_ref=field_y.at[index], dst_ref=halo.at[slot],
            send_sem=send_h.at[slot], recv_sem=recv_h.at[slot],
            device_id={"energy": seat + 1}, device_id_type=MESH,
        )

    def halo_down(index):
        slot = index + REACH
        return pltpu.make_async_remote_copy(
            src_ref=field_y.at[index], dst_ref=halo.at[slot],
            send_sem=send_h.at[slot], recv_sem=recv_h.at[slot],
            device_id={"energy": seat - 1}, device_id_type=MESH,
        )

    def closing(which, halves):
        result = matmul((hops[which, 2], hops[which, 3]), join(halves, 0))
        left[0], left[1] = result[:, :width], result[:, width:]

    def contact(index, which):
        @pl.when((which == 0) & has_prev)
        def _():
            halves = []
            for part in range(CHUNKS):
                forward_copy(0, index, part).wait_recv()
                rows = slice(edges[part], edges[part + 1])
                field = [split(came_f[index, side, rows]) for side in range(2)]
                half = matmul(join(field, 0), (hops[0, 0], hops[0, 1]))
                size = edges[part + 1] - edges[part]
                halves.append(join([split(half[:size]), split(half[size:])], 1))
            closing(0, halves)

        @pl.when(which == 1)
        def _():
            field = [split(local[0, index, side]) for side in range(2)]
            half = matmul(join(field, 0), (hops[1, 0], hops[1, 1]))
            closing(1, [join([split(half[:width]), split(half[width:])], 1)])

    def inverse(index, which, step):
        number = jnp.full((1, width), 2 * (seat * count + index) + 1, jnp.int32)
        energy = -1.0 + number.astype(F32) / (count * spans)
        sys_re = jnp.where(eye, energy, 0.0) - hamil[which] - sigma[which, index, 0] - left[0]
        sys_im = jnp.where(eye, ETA, 0.0) - sigma[which, index, 1] - left[1]
        diag_re = jnp.where(eye, sys_re, 0.0)
        diag_im = jnp.where(eye, sys_im, 0.0)
        inverses = []
        for axis in (1, 0):
            real_c = jnp.sum(diag_re, axis=axis, keepdims=True)
            imag_c = jnp.sum(diag_im, axis=axis, keepdims=True)
            modulus = real_c * real_c + imag_c * imag_c
            inverses.append((real_c / modulus, -imag_c / modulus))
        (col_re, col_im), (row_re, row_im) = inverses
        rest_re = jnp.where(eye, 0.0, sys_im * row_im - sys_re * row_re)
        rest_im = jnp.where(eye, 0.0, -(sys_re * row_im + sys_im * row_re))
        square_re, square_im = complex_matmul((rest_re, rest_im), (rest_re, rest_im))
        powers_re, powers_im = complex_matmul(
            (jnp.concatenate([rest_re, square_re], 0), jnp.concatenate([rest_im, square_im], 0)),
            (square_re, square_im),
        )
        sum_re = jnp.where(eye, 1.0, 0.0) + rest_re + square_re + powers_re[:width]
        sum_im = rest_im + square_im + powers_im[:width]
        base_re = col_re * sum_re - col_im * sum_im
        base_im = col_re * sum_im + col_im * sum_re
        out_re, out_im = complex_matmul((base_re, base_im), (powers_re[width:], powers_im[width:]))
        local[which, index, 0] = base_re + out_re
        local[which, index, 1] = base_im + out_im
        if paced:
            @pl.when(pacing & ((step > 0) | odd))
            def _():
                pl.semaphore_wait(turns, 1)

        @pl.when(has_next & ((place < fold) | (which == 1)))
        def _():
            for part in range(CHUNKS):
                forward_copy(which, index, part).start()

        if paced:
            @pl.when(pacing & ((step < count - 1) | (core == 0)))
            def _():
                forward_copy(which, index, CHUNKS - 2).wait_send()
                pl.semaphore_signal(turns, inc=1, device_id=partner, device_id_type=MESH)

    def forward(step):
        index = order(step)
        load(index).wait()

        def slab(which, carry):
            @pl.when(which == 1)
            def _():
                give(index).wait_recv()

            contact(index, which)
            inverse(index, which, step)
            return carry

        slabs = jnp.where(folding & has_next, 2, 1)
        lax.fori_loop(0, slabs, slab, 0)

    def finish(index):
        field = join([split(green[index, 0, side]) for side in range(2)], 0)
        half = matmul(field, (mats[2], mats[3]))
        half = join([split(half[:width]), split(half[width:])], 1)
        result = matmul((mats[0], mats[1]), half)
        field_y[index, 0] = result[:, :width]
        field_y[index, 1] = result[:, width:]

        @pl.when(has_high & (index >= count - REACH))
        def _():
            halo_up(index).start()

        @pl.when(has_low & (index < REACH))
        def _():
            halo_down(index).start()

    def send_back(index, out_re, out_im):
        sent_b[index, 0] = out_re
        sent_b[index, 1] = out_im
        for part in range(CHUNKS):
            backward_copy(index, part).start()

    def backward(index):
        @pl.when(has_prev)
        def _():
            base = [split(local[0, index, side]) for side in range(2)]
            lefts = matmul((hops[0, 0], hops[0, 1]), join(base, 1))
            rights = matmul(join(base, 0), (hops[0, 2], hops[0, 3]))
            lefts = splits(lefts[:, :width], lefts[:, width:])
            columns = complex_columns(splits(rights[:width], rights[width:]))
            whole = matmul(join(lefts, 0), (hops[0, 2], hops[0, 3]))
            lefts = complex_rows(lefts)
            mids = []
            for part in range(CHUNKS):
                backward_copy(index, part).wait_recv()
                rows = slice(edges[part], edges[part + 1])
                incoming = join([split(came_b[index, side, rows]) for side in range(2)], 1)
                mids.append(matmul(incoming, columns))
            mid = jnp.concatenate(mids, axis=0)
            columns = complex_columns(splits(mid[:, :width], mid[:, width:]))
            out = matmul(lefts, columns)
            send_back(index, whole[:width] + out[:, :width], whole[width:] + out[:, width:])

        base_re, base_im = local[0, index, 0], local[0, index, 1]
        base = splits(base_re, base_im)
        columns = complex_columns(base)
        mids = []
        for part in range(CHUNKS):
            @pl.when(jnp.logical_not(has_prev))
            def _():
                backward_copy(index, part).wait_recv()

            rows = slice(edges[part], edges[part + 1])
            incoming = join([split(came_b[index, side, rows]) for side in range(2)], 1)
            mids.append(matmul(incoming, columns))
        mid = jnp.concatenate(mids, axis=0)
        out = matmul(complex_rows(base), complex_columns(splits(mid[:, :width], mid[:, width:])))
        green[index, 0, 0] = base_re + out[:, :width]
        green[index, 0, 1] = base_im + out[:, width:]
        finish(index)

    def refold(index):
        far_end = [split(local[1, index, side]) for side in range(2)]
        half = matmul((hops[1, 0], hops[1, 1]), join(far_end, 1))
        half = join([split(half[:, :width]), split(half[:, width:])], 0)
        incoming = matmul(half, (hops[1, 2], hops[1, 3]))
        base = local[0, index, 0], local[0, index, 1]
        mid = complex_matmul((incoming[:width], incoming[width:]), base)
        out_re, out_im = complex_matmul(base, mid)
        out_re, out_im = base[0] + out_re, base[1] + out_im
        green[index, 0, 0] = out_re
        green[index, 0, 1] = out_im

        @pl.when(has_prev)
        def _():
            full = join(splits(out_re, out_im), 1)
            half = matmul((hops[0, 0], hops[0, 1]), full)
            half = join([split(half[:, :width]), split(half[:, width:])], 0)
            out = matmul(half, (hops[0, 2], hops[0, 3]))
            send_back(index, out[:width], out[width:])

        finish(index)

    def receive(index):
        for part in range(CHUNKS):
            forward_copy(0, index, part).wait_recv()
        green[index, 0] = came_f[index]
        finish(index)

    behind = 2 * (fold - place)

    def turn(step, carry):
        @pl.when((place <= fold) & (step < count))
        def _():
            forward(step)

        @pl.when((step == 0) & jnp.logical_not(has_prev))
        def _():
            set_mats()

        @pl.when((place < fold) & (step >= behind) & (step < behind + count))
        def _():
            backward(order(step - behind))

        @pl.when(folding & has_next & (step < count))
        def _():
            refold(order(step))

        @pl.when(leaf & has_prev & (step < count))
        def _():
            receive(order(step))

        return carry

    lax.fori_loop(0, count + 2 * fold, turn, 0)

    near = jnp.float32(0.0)
    far = jnp.float32(0.0)
    for mode in range(offsets.shape[0]):
        near = near + jnp.where(offsets[mode] == 1, strength[mode], 0.0)
        far = far + jnp.where(offsets[mode] == 2, strength[mode], 0.0)

    @pl.when(has_high)
    def _():
        for slot in range(REACH):
            halo_down(slot).wait_recv()

    @pl.when(has_low)
    def _():
        for slot in range(REACH):
            halo_up(count - REACH + slot).wait_recv()

    def block(index, side):
        if index < 0:
            return halo[index + REACH, side]
        if index >= count:
            return halo[index - count + REACH, side]
        return field_y[index, side]

    for index in range(count):
        for side in range(2):
            self_out[index, 0, side] = near * (
                block(index - 1, side) + block(index + 1, side)
            ) + far * (block(index - 2, side) + block(index + 2, side))

    @pl.when(has_next)
    def _():
        for step in range(count):
            for part in range(CHUNKS):
                if paced and part == CHUNKS - 2:
                    waited = pacing & ((step < count - 1) | (core == 0))

                    @pl.when(jnp.logical_not(waited))
                    def _():
                        forward_copy(0, order(step), part).wait_send()
                else:
                    forward_copy(0, order(step), part).wait_send()

    @pl.when(has_prev & (place < last))
    def _():
        for index in range(count):
            for part in range(CHUNKS):
                backward_copy(index, part).wait_send()

    @pl.when(leaf & has_prev)
    def _():
        give_shared().wait_send()
        for index in range(count):
            give(index).wait_send()

    @pl.when(folding & has_next)
    def _():
        give_partner().wait_send()

    @pl.when(has_high)
    def _():
        for slot in range(REACH):
            halo_up(count - REACH + slot).wait_send()

    @pl.when(has_low)
    def _():
        for slot in range(REACH):
            halo_down(slot).wait_send()


def per_device(self_in, onsite, within, between, coupling, groups, offsets, strength):
    count, width = self_in.shape[0], self_in.shape[3]
    smem = pl.BlockSpec(memory_space=pltpu.SMEM)
    vmem = pl.BlockSpec(memory_space=pltpu.VMEM)
    hbm = pl.BlockSpec(memory_space=pltpu.HBM)
    shape = jax.ShapeDtypeStruct(self_in.shape, F32)
    dma = pltpu.SemaphoreType.DMA
    blocks = pltpu.VMEM((count, 2, width, width), F32)
    return pl.pallas_call(
        kernel,
        out_shape=(shape, shape),
        in_specs=[smem] * 2 + [hbm] * 6,
        out_specs=(vmem, vmem),
        scratch_shapes=[
            pltpu.VMEM(onsite.shape, F32),
            pltpu.VMEM(within.shape, F32),
            pltpu.VMEM(between.shape, F32),
            pltpu.VMEM(coupling.shape, F32),
            pltpu.VMEM(groups.shape, jnp.int32),
            dma((5,)),
            pltpu.VMEM((2, width, width), F32),
            pltpu.VMEM((2, 4, width, width), BF16),
            pltpu.VMEM((4, width, width), BF16),
            pltpu.VMEM((2, width, width), F32),
            pltpu.VMEM((2, count, 2, width, width), F32),
            pltpu.VMEM((2, count, 2, width, width), F32),
            blocks, blocks, blocks,
            pltpu.VMEM((4, width, width), F32),
            blocks,
            pltpu.VMEM((2 * REACH, 2, width, width), F32),
            dma((count,)),
            dma((count, CHUNKS)), dma((count, CHUNKS)), dma((count, CHUNKS)), dma((count, CHUNKS)),
            dma((2 * REACH,)), dma((2 * REACH,)),
            dma((count,)), dma((count,)), dma((2,)), dma((2,)),
            pltpu.SemaphoreType.REGULAR,
        ],
        compiler_params=pltpu.CompilerParams(
            collective_id=0, has_side_effects=True, vmem_limit_bytes=60 * 2**20
        ),
    )(offsets, strength, self_in, onsite, within, between, coupling, groups)


def solution(mesh):
    placed = (
        P("energy", "section", None, None, None),
        P("section", None),
        P("section", None, None),
        P("section", None, None),
        P("section", None, None),
        P("section", None),
        P(),
        P(),
    )
    return jax.shard_map(
        per_device,
        mesh=mesh,
        in_specs=placed,
        out_specs=(
            P("energy", "section", None, None, None),
            P("energy", "section", None, None, None),
        ),
        check_vma=False,
    )
```

```python
import jax
import jax.numpy as jnp
from jax import lax
from jax.experimental import pallas as pl
from jax.experimental.pallas import tpu as pltpu
from jax.sharding import PartitionSpec as P

ETA = 1.0
CONTACT = 0.6
REACH = 2
CHUNKS = 2
CUT = 4

F32 = jnp.float32
BF16 = jnp.bfloat16
MESH = pl.DeviceIdType.MESH


def split(value):
    high = value.astype(BF16)
    return high, (value - high.astype(F32)).astype(BF16)


def join(pieces, axis):
    return tuple(jnp.concatenate(parts, axis=axis) for parts in zip(*pieces))


def dot(left, right):
    return jnp.dot(left, right, preferred_element_type=F32)


def matmul(left, right):
    (left_h, left_l), (right_h, right_l) = left, right
    return dot(left_h, right_h) + (dot(left_h, right_l) + dot(left_l, right_h))


def minus(pair):
    return tuple(-part for part in pair)


def complex_columns(block):
    return join([join([block[0], block[1]], 1), join([minus(block[1]), block[0]], 1)], 0)


def complex_rows(block):
    return join(block, 1)


def splits(real, imag):
    return split(real), split(imag)


def complex_matmul(left, right):
    first = matmul(split(left[0]), split(right[0]))
    second = matmul(split(left[1]), split(right[1]))
    third = matmul(split(left[0] + left[1]), split(right[0] + right[1]))
    return first - second, third - first - second


def kernel(
    self_in, onsite_in, within_in, between_in, coupling_in, groups_in,
    green_out, fields_out,
    green, keep_g, keep_y, keep_h,
    onsite, within, between, coupling, groups, load_p,
    ready_l, ready_r, ready_w, hamil, hops, mats, outer, left, sigma, local, came_f, came_b, sent_b, given, field_y, halo,
    load_s, send_f, recv_f, send_b, recv_b, send_h, recv_h, send_x, recv_x, send_g, recv_g,
    turns,
):
    count, width = self_in.shape[0], self_in.shape[3]
    sections, place = lax.axis_size("section"), lax.axis_index("section")
    spans, seat = lax.axis_size("energy"), lax.axis_index("energy")
    last = sections - 1
    fold = max(sections - 2, 0)
    has_prev, has_next = place > 0, place < last
    has_low, has_high = seat > 0, seat < spans - 1
    folding, leaf = place == fold, place == last
    edges = (0, width - width // CUT, width)
    spans_of = tuple(zip(edges[:-1], edges[1:]))
    core = lax.rem(seat, 2)
    odd = core == 1
    partner = {"energy": seat + 1 - 2 * core}
    paced = sections > 2
    pacing = (place == 0) if paced else (place < 0)

    def order(step):
        return jnp.where(odd, count - 1 - step, step)

    def load(index):
        return pltpu.make_async_copy(self_in.at[index, 0], sigma.at[0, index], load_s.at[index])

    params = [
        pltpu.make_async_copy(source, target, load_p.at[number])
        for number, (source, target) in enumerate(
            (
                (between_in, between), (within_in, within), (onsite_in, onsite),
                (groups_in, groups), (coupling_in, coupling),
            )
        )
    ]
    for param in params[:3]:
        param.start()
    for step in range(count):
        load(order(step)).start()
    for param in params[3:]:
        param.start()

    barrier = pltpu.get_barrier_semaphore()
    for present, target in (
        (has_prev, {"section": place - 1}),
        (has_next, {"section": place + 1}),
        (has_low, {"energy": seat - 1}),
        (has_high, {"energy": seat + 1}),
    ):
        @pl.when(present)
        def _():
            pl.semaphore_signal(barrier, inc=1, device_id=target, device_id_type=MESH)

    eye = (
        lax.broadcasted_iota(jnp.int32, (width, width), 0)
        == lax.broadcasted_iota(jnp.int32, (width, width), 1)
    )
    for param in params[:3]:
        param.wait()
    hop = between[0]
    own = jnp.where(eye, onsite[0:1, :], 0.0) + 0.5 * (within[0] + within[0].T)
    hamil[0] = own
    given[0] = hop
    given[1] = own

    def give(index):
        return pltpu.make_async_remote_copy(
            src_ref=sigma.at[0, index], dst_ref=sigma.at[1, index],
            send_sem=send_x.at[index], recv_sem=recv_x.at[index],
            device_id={"section": place - 1}, device_id_type=MESH,
        )

    def give_shared():
        return pltpu.make_async_remote_copy(
            src_ref=given.at[core], dst_ref=given.at[2 + core],
            send_sem=send_g.at[0], recv_sem=recv_g.at[0],
            device_id={"section": place - 1}, device_id_type=MESH,
        )

    def give_partner():
        return pltpu.make_async_remote_copy(
            src_ref=given.at[2 + core], dst_ref=given.at[2 + core],
            send_sem=send_g.at[1], recv_sem=recv_g.at[1],
            device_id=partner, device_id_type=MESH,
        )

    def set_hops(which, value):
        hops[which, 0], hops[which, 1] = split(value)
        hops[which, 2], hops[which, 3] = split(value.T)

    set_hops(0, hop)

    @pl.when(seat == 0)
    def _():
        halo[0:REACH] = jnp.zeros((REACH, 2, width, width), F32)

    @pl.when(seat == spans - 1)
    def _():
        halo[REACH : 2 * REACH] = jnp.zeros((REACH, 2, width, width), F32)

    @pl.when(place == 0)
    def _():
        left[0] = jnp.zeros((width, width), F32)
        left[1] = -CONTACT * matmul((hops[0, 2], hops[0, 3]), (hops[0, 0], hops[0, 1]))

    def set_mats():
        for param in params[3:]:
            param.wait()
        row_group = jnp.broadcast_to(groups[0:1, :].astype(F32), (width, width))
        mat = jnp.where(row_group == row_group.T, coupling[0], 0.0)
        mats[0], mats[1] = split(mat)
        mats[2], mats[3] = split(mat.T)
        outer[...] = mats[...]

        @pl.when(has_prev)
        def _():
            outer[...] = hops[0]


    def inverse(index, which, left_re, left_im):
        number = jnp.full((1, width), 2 * (seat * count + index) + 1, jnp.int32)
        energy = -1.0 + number.astype(F32) / (count * spans)
        sys_re = jnp.where(eye, energy, 0.0) - hamil[which] - sigma[which, index, 0] - left_re
        sys_im = jnp.where(eye, ETA, 0.0) - sigma[which, index, 1] - left_im
        diag_re = jnp.where(eye, sys_re, 0.0)
        diag_im = jnp.where(eye, sys_im, 0.0)
        inverses = []
        for axis in (1, 0):
            real_c = jnp.sum(diag_re, axis=axis, keepdims=True)
            imag_c = jnp.sum(diag_im, axis=axis, keepdims=True)
            modulus = real_c * real_c + imag_c * imag_c
            inverses.append((real_c / modulus, -imag_c / modulus))
        (col_re, col_im), (row_re, row_im) = inverses
        rest_re = jnp.where(eye, 0.0, sys_im * row_im - sys_re * row_re)
        rest_im = jnp.where(eye, 0.0, -(sys_re * row_im + sys_im * row_re))
        square_re, square_im = complex_matmul((rest_re, rest_im), (rest_re, rest_im))
        powers_re, powers_im = complex_matmul(
            (jnp.concatenate([rest_re, square_re], 0), jnp.concatenate([rest_im, square_im], 0)),
            (square_re, square_im),
        )
        sum_re = jnp.where(eye, 1.0, 0.0) + rest_re + square_re + powers_re[:width]
        sum_im = rest_im + square_im + powers_im[:width]
        base_re = col_re * sum_re - col_im * sum_im
        base_im = col_re * sum_im + col_im * sum_re
        out_re, out_im = complex_matmul((base_re, base_im), (powers_re[width:], powers_im[width:]))
        return base_re + out_re, base_im + out_im

    def invert(index):
        local[0, index, 0], local[0, index, 1] = inverse(index, 0, left[0], left[1])

    if paced:
        @pl.when(pacing)
        def _():
            load(order(0)).wait()
            invert(order(0))

    peers = sum(present.astype(jnp.int32) for present in (has_prev, has_next, has_low, has_high))
    pl.semaphore_wait(barrier, peers)

    @pl.when(leaf & has_prev)
    def _():
        give_shared().start()
        for step in range(count):
            index = order(step)
            load(index).wait()
            give(index).start()

    @pl.when(has_prev)
    def _():
        set_mats()

    @pl.when(folding & has_next)
    def _():
        give_shared().wait_recv()
        give_partner().start()
        give_partner().wait_recv()
        set_hops(1, given[2])
        hamil[1] = given[3]

    def forward_copy(which, index, part):
        rows = pl.ds(edges[part], edges[part + 1] - edges[part])
        return pltpu.make_async_remote_copy(
            src_ref=local.at[which, index, :, rows], dst_ref=came_f.at[index, :, rows],
            send_sem=send_f.at[index, part], recv_sem=recv_f.at[index, part],
            device_id={"section": place + 1}, device_id_type=MESH,
        )

    def backward_copy(index, part):
        rows = pl.ds(edges[part], edges[part + 1] - edges[part])
        return pltpu.make_async_remote_copy(
            src_ref=sent_b.at[index, :, rows], dst_ref=came_b.at[index, :, rows],
            send_sem=send_b.at[index, part], recv_sem=recv_b.at[index, part],
            device_id={"section": place - 1}, device_id_type=MESH,
        )

    def halo_up(index):
        slot = index - (count - REACH)
        return pltpu.make_async_remote_copy(
            src_ref=field_y.at[index], dst_ref=halo.at[slot],
            send_sem=send_h.at[slot], recv_sem=recv_h.at[slot],
            device_id={"energy": seat + 1}, device_id_type=MESH,
        )

    def halo_down(index):
        slot = index + REACH
        return pltpu.make_async_remote_copy(
            src_ref=field_y.at[index], dst_ref=halo.at[slot],
            send_sem=send_h.at[slot], recv_sem=recv_h.at[slot],
            device_id={"energy": seat - 1}, device_id_type=MESH,
        )

    def contact(index):
        halves = []
        for part in range(CHUNKS):
            forward_copy(0, index, part).wait_recv()
            rows = slice(edges[part], edges[part + 1])
            field = [split(came_f[index, side, rows]) for side in range(2)]
            half = matmul(join(field, 0), (hops[0, 0], hops[0, 1]))
            size = edges[part + 1] - edges[part]
            halves.append(join([split(half[:size]), split(half[size:])], 1))
        result = matmul((hops[0, 2], hops[0, 3]), join(halves, 0))
        left[0], left[1] = result[:, :width], result[:, width:]

    def launch(index, which):
        for part in range(CHUNKS):
            forward_copy(which, index, part).start()

    def forward(step):
        ahead = step
        if paced:
            ahead = step + pacing.astype(jnp.int32)

            @pl.when(pacing)
            def _():
                @pl.when((step > 0) | odd)
                def _():
                    pl.semaphore_wait(turns, 1)

                launch(order(step), 0)

        @pl.when(ahead < count)
        def _():
            index = order(ahead)
            load(index).wait()

            @pl.when(has_prev)
            def _():
                contact(index)

            invert(index)

            @pl.when(jnp.logical_not(pacing) & (place < fold))
            def _():
                launch(index, 0)

        if paced:
            @pl.when(pacing & ((step < count - 1) | (core == 0)))
            def _():
                forward_copy(0, order(step), CHUNKS - 2).wait_send()
                pl.semaphore_signal(turns, inc=1, device_id=partner, device_id_type=MESH)

    def publish(index):
        return pltpu.make_async_copy(green.at[index], green_out.at[index], keep_g.at[index])

    def publish_field(index):
        return pltpu.make_async_copy(field_y.at[index], fields_out.at[index + REACH], keep_y.at[index])

    def publish_halo(slot):
        target = slot if slot < REACH else slot + count
        return pltpu.make_async_copy(halo.at[slot], fields_out.at[target], keep_h.at[slot])

    def neighbours(index):
        publish_field(index).start()

        @pl.when(has_high & (index >= count - REACH))
        def _():
            halo_up(index).start()

        @pl.when(has_low & (index < REACH))
        def _():
            halo_down(index).start()

    def finish(index):
        field = join([split(green[index, 0, side]) for side in range(2)], 0)
        half = matmul(field, (mats[2], mats[3]))
        half = join([split(half[:width]), split(half[width:])], 1)
        result = matmul((mats[0], mats[1]), half)
        field_y[index, 0] = result[:, :width]
        field_y[index, 1] = result[:, width:]
        neighbours(index)

    def send_back(index, out_re, out_im):
        sent_b[index, 0] = out_re
        sent_b[index, 1] = out_im
        for part in range(CHUNKS):
            backward_copy(index, part).start()

    def prepare(index):
        base = [split(local[0, index, side]) for side in range(2)]
        lefts = matmul((outer[0], outer[1]), join(base, 1))
        rights = matmul(join(base, 0), (outer[2], outer[3]))
        lefts = splits(lefts[:, :width], lefts[:, width:])
        ready_r[0], ready_r[1] = complex_columns(splits(rights[:width], rights[width:]))
        ready_w[...] = matmul(join(lefts, 0), (outer[2], outer[3]))
        ready_l[0], ready_l[1] = complex_rows(lefts)

    def backward(index):
        columns = ready_r[0], ready_r[1]
        mids = []
        for part in range(CHUNKS):
            backward_copy(index, part).wait_recv()
            rows = slice(edges[part], edges[part + 1])
            incoming = join([split(came_b[index, side, rows]) for side in range(2)], 1)
            mids.append(matmul(incoming, columns))
        mid = jnp.concatenate(mids, axis=0)
        out = matmul((ready_l[0], ready_l[1]), complex_columns(splits(mid[:, :width], mid[:, width:])))
        out_re, out_im = ready_w[:width] + out[:, :width], ready_w[width:] + out[:, width:]

        @pl.when(has_prev)
        def _():
            send_back(index, out_re, out_im)

        @pl.when(jnp.logical_not(has_prev))
        def _():
            field_y[index, 0] = out_re
            field_y[index, 1] = out_im
            neighbours(index)

        base_re, base_im = local[0, index, 0], local[0, index, 1]
        mid = complex_matmul((came_b[index, 0], came_b[index, 1]), (base_re, base_im))
        out_re, out_im = complex_matmul((base_re, base_im), mid)
        green[index, 0, 0] = base_re + out_re
        green[index, 0, 1] = base_im + out_im
        publish(index).start()

        @pl.when(has_prev)
        def _():
            finish(index)

    def refold(index):
        give(index).wait_recv()
        base_re, base_im = local[0, index, 0], local[0, index, 1]
        base = splits(base_re, base_im)
        half = matmul(join(base, 0), (hops[1, 0], hops[1, 1]))
        half_re, half_im = half[:width], half[width:]
        half = join(splits(half_re, half_im), 1)
        result = matmul((hops[1, 2], hops[1, 3]), half)
        end_re, end_im = inverse(index, 1, result[:, :width], result[:, width:])
        outer_l = matmul((hops[0, 0], hops[0, 1]), half)
        inner_r = matmul((hops[1, 2], hops[1, 3]), join(base, 1))
        inner_re, inner_im = inner_r[:, :width], inner_r[:, width:]
        outer_r = matmul(join(splits(inner_re, inner_im), 0), (hops[0, 2], hops[0, 3]))
        whole = matmul((hops[0, 0], hops[0, 1]), join(base, 1))
        whole = join(splits(whole[:, :width], whole[:, width:]), 0)
        whole = matmul(whole, (hops[0, 2], hops[0, 3]))
        mid = complex_matmul((end_re, end_im), (outer_r[:width], outer_r[width:]))
        out_re, out_im = complex_matmul((outer_l[:, :width], outer_l[:, width:]), mid)
        local[1, index, 0], local[1, index, 1] = end_re, end_im

        @pl.when(has_prev)
        def _():
            send_back(index, whole[:width] + out_re, whole[width:] + out_im)

        launch(index, 1)
        mid = complex_matmul((local[1, index, 0], local[1, index, 1]), (inner_re, inner_im))
        out_re, out_im = complex_matmul((half_re, half_im), mid)
        green[index, 0, 0] = local[0, index, 0] + out_re
        green[index, 0, 1] = local[0, index, 1] + out_im
        publish(index).start()
        finish(index)

    def receive(index):
        for part in range(CHUNKS):
            forward_copy(0, index, part).wait_recv()
        green[index, 0] = came_f[index]
        publish(index).start()
        finish(index)

    behind = 2 * (fold - place)

    def turn(step, carry):
        @pl.when((place <= fold) & (step < count))
        def _():
            forward(step)

        @pl.when((step == 0) & jnp.logical_not(has_prev))
        def _():
            set_mats()

        @pl.when((place < fold) & (step >= behind) & (step < behind + count))
        def _():
            backward(order(step - behind))

        @pl.when((place < fold) & (step + 1 >= behind) & (step + 1 < behind + count))
        def _():
            prepare(order(step + 1 - behind))

        @pl.when(folding & has_next & (step < count))
        def _():
            refold(order(step))

        @pl.when(leaf & has_prev & (step < count))
        def _():
            receive(order(step))

        return carry

    lax.fori_loop(0, count + 2 * fold, turn, 0)

    @pl.when(has_low)
    def _():
        for slot in range(REACH):
            halo_up(count - REACH + slot).wait_recv()

    for slot in range(REACH):
        publish_halo(slot).start()

    @pl.when(has_high)
    def _():
        for slot in range(REACH):
            halo_down(slot).wait_recv()

    for slot in range(REACH):
        publish_halo(REACH + slot).start()

    @pl.when(has_next)
    def _():
        for step in range(count):
            for part in range(CHUNKS):
                if paced and part == CHUNKS - 2:
                    waited = pacing & ((step < count - 1) | (core == 0))

                    @pl.when(jnp.logical_not(waited))
                    def _():
                        forward_copy(0, order(step), part).wait_send()
                else:
                    forward_copy(0, order(step), part).wait_send()

    @pl.when(has_prev & (place < last))
    def _():
        for index in range(count):
            for part in range(CHUNKS):
                backward_copy(index, part).wait_send()

    @pl.when(leaf & has_prev)
    def _():
        give_shared().wait_send()
        for index in range(count):
            give(index).wait_send()

    @pl.when(folding & has_next)
    def _():
        give_partner().wait_send()

    @pl.when(has_high)
    def _():
        for slot in range(REACH):
            halo_up(count - REACH + slot).wait_send()

    @pl.when(has_low)
    def _():
        for slot in range(REACH):
            halo_down(slot).wait_send()

    for index in range(count):
        publish(index).wait()
        publish_field(index).wait()
    for slot in range(2 * REACH):
        publish_halo(slot).wait()


def combine(offsets, strength, green, fields, green_out, self_out, held, block, total, load_g, load_f, save_g, save_s):
    count = green.shape[0]
    loads = [
        pltpu.make_async_copy(fields.at[slot], block.at[slot], load_f.at[slot])
        for slot in range(count + 2 * REACH)
    ]
    brings = [pltpu.make_async_copy(green.at[index], held.at[index], load_g.at[index]) for index in range(count)]
    keeps = [pltpu.make_async_copy(held.at[index], green_out.at[index], save_g.at[index]) for index in range(count)]
    saves = [pltpu.make_async_copy(total.at[index], self_out.at[index], save_s.at[index]) for index in range(count)]
    for copy in brings + loads:
        copy.start()
    near = jnp.float32(0.0)
    far = jnp.float32(0.0)
    for mode in range(offsets.shape[0]):
        near = near + jnp.where(offsets[mode] == 1, strength[mode], 0.0)
        far = far + jnp.where(offsets[mode] == 2, strength[mode], 0.0)
    for bring, keep in zip(brings, keeps):
        bring.wait()
        keep.start()
    arrived = 0
    for index in range(count):
        while arrived <= index + 2 * REACH:
            loads[arrived].wait()
            arrived += 1
        middle = index + REACH
        total[index, 0] = near * (block[middle - 1] + block[middle + 1]) + far * (
            block[middle - 2] + block[middle + 2]
        )
        saves[index].start()
    for copy in keeps + saves:
        copy.wait()


def per_device(self_in, onsite, within, between, coupling, groups, offsets, strength):
    count, width = self_in.shape[0], self_in.shape[3]
    smem = pl.BlockSpec(memory_space=pltpu.SMEM)
    hbm = pl.BlockSpec(memory_space=pltpu.HBM)
    shape = jax.ShapeDtypeStruct(self_in.shape, F32)
    dma = pltpu.SemaphoreType.DMA
    blocks = pltpu.VMEM((count, 2, width, width), F32)
    fields = jax.ShapeDtypeStruct((count + 2 * REACH, 2, width, width), F32)
    green, fields = pl.pallas_call(
        kernel,
        out_shape=(shape, fields),
        in_specs=[hbm] * 6,
        out_specs=(hbm, hbm),
        scratch_shapes=[
            pltpu.VMEM(self_in.shape, F32),
            dma((count,)), dma((count,)), dma((2 * REACH,)),
            pltpu.VMEM(onsite.shape, F32),
            pltpu.VMEM(within.shape, F32),
            pltpu.VMEM(between.shape, F32),
            pltpu.VMEM(coupling.shape, F32),
            pltpu.VMEM(groups.shape, jnp.int32),
            dma((5,)),
            pltpu.VMEM((2, width, 2 * width), BF16),
            pltpu.VMEM((2, 2 * width, 2 * width), BF16),
            pltpu.VMEM((2 * width, width), F32),
            pltpu.VMEM((2, width, width), F32),
            pltpu.VMEM((2, 4, width, width), BF16),
            pltpu.VMEM((4, width, width), BF16),
            pltpu.VMEM((4, width, width), BF16),
            pltpu.VMEM((2, width, width), F32),
            pltpu.VMEM((2, count, 2, width, width), F32),
            pltpu.VMEM((2, count, 2, width, width), F32),
            blocks, blocks, blocks,
            pltpu.VMEM((4, width, width), F32),
            blocks,
            pltpu.VMEM((2 * REACH, 2, width, width), F32),
            dma((count,)),
            dma((count, CHUNKS)), dma((count, CHUNKS)), dma((count, CHUNKS)), dma((count, CHUNKS)),
            dma((2 * REACH,)), dma((2 * REACH,)),
            dma((count,)), dma((count,)), dma((2,)), dma((2,)),
            pltpu.SemaphoreType.REGULAR,
        ],
        compiler_params=pltpu.CompilerParams(
            collective_id=0, has_side_effects=True, vmem_limit_bytes=60 * 2**20
        ),
    )(self_in, onsite, within, between, coupling, groups)
    return pl.pallas_call(
        combine,
        out_shape=(shape, shape),
        in_specs=[smem] * 2 + [hbm] * 2,
        out_specs=(hbm, hbm),
        scratch_shapes=[
            pltpu.VMEM(self_in.shape, F32),
            pltpu.VMEM((count + 2 * REACH, 2, width, width), F32),
            pltpu.VMEM(self_in.shape, F32),
            dma((count,)), dma((count + 2 * REACH,)), dma((count,)), dma((count,)),
        ],
        compiler_params=pltpu.CompilerParams(vmem_limit_bytes=60 * 2**20),
    )(offsets, strength, green, fields)


def solution(mesh):
    placed = (
        P("energy", "section", None, None, None),
        P("section", None),
        P("section", None, None),
        P("section", None, None),
        P("section", None, None),
        P("section", None),
        P(),
        P(),
    )
    return jax.shard_map(
        per_device,
        mesh=mesh,
        in_specs=placed,
        out_specs=(
            P("energy", "section", None, None, None),
            P("energy", "section", None, None, None),
        ),
        check_vma=False,
    )
```

```python
import jax
import jax.numpy as jnp
from jax import lax
from jax.experimental import pallas as pl
from jax.experimental.pallas import tpu as pltpu
from jax.sharding import PartitionSpec as P

ETA = 1.0
CONTACT = 0.6
REACH = 2
CHUNKS = 2

F32 = jnp.float32
BF16 = jnp.bfloat16
MESH = pl.DeviceIdType.MESH


def split(value):
    high = value.astype(BF16)
    return high, (value - high.astype(F32)).astype(BF16)


def join(pieces, axis):
    return tuple(jnp.concatenate(parts, axis=axis) for parts in zip(*pieces))


def dot(left, right):
    return jnp.dot(left, right, preferred_element_type=F32)


def matmul(left, right):
    (left_h, left_l), (right_h, right_l) = left, right
    return dot(left_h, right_h) + (dot(left_h, right_l) + dot(left_l, right_h))


def minus(pair):
    return tuple(-part for part in pair)


def complex_columns(block):
    return join([join([block[0], block[1]], 1), join([minus(block[1]), block[0]], 1)], 0)


def complex_rows(block):
    return join(block, 1)


def splits(real, imag):
    return split(real), split(imag)


def complex_matmul(left, right):
    first = matmul(split(left[0]), split(right[0]))
    second = matmul(split(left[1]), split(right[1]))
    third = matmul(split(left[0] + left[1]), split(right[0] + right[1]))
    return first - second, third - first - second


def kernel(
    self_in, onsite_in, within_in, between_in, coupling_in, groups_in,
    green_out, fields_out,
    green, keep_g, keep_y, keep_h,
    onsite, within, between, coupling, groups, load_p,
    ready_l, ready_r, ready_w, hamil, hops, mats, outer, left, sigma, local, came_f, came_b, sent_b, given, field_y, halo,
    load_s, send_f, recv_f, send_b, recv_b, send_h, recv_h, send_x, recv_x, send_g, recv_g,
    turns,
):
    count, width = self_in.shape[0], self_in.shape[3]
    sections, place = lax.axis_size("section"), lax.axis_index("section")
    spans, seat = lax.axis_size("energy"), lax.axis_index("energy")
    last = sections - 1
    fold = max(sections - 2, 0)
    has_prev, has_next = place > 0, place < last
    has_low, has_high = seat > 0, seat < spans - 1
    folding, leaf = place == fold, place == last
    edges = (0, width * 13 // 16 // 16 * 16, width)
    spans_of = tuple(zip(edges[:-1], edges[1:]))
    core = lax.rem(seat, 2)
    odd = core == 1
    partner = {"energy": seat + 1 - 2 * core}
    paced = sections > 2
    pacing = (place == 0) if paced else (place < 0)

    def order(step):
        return jnp.where(odd, count - 1 - step, step)

    def load(index):
        return pltpu.make_async_copy(self_in.at[index, 0], sigma.at[0, index], load_s.at[index])

    params = [
        pltpu.make_async_copy(source, target, load_p.at[number])
        for number, (source, target) in enumerate(
            (
                (between_in, between), (within_in, within), (onsite_in, onsite),
                (groups_in, groups), (coupling_in, coupling),
            )
        )
    ]
    for param in params[:3]:
        param.start()
    for step in range(count):
        load(order(step)).start()
    for param in params[3:]:
        param.start()

    barrier = pltpu.get_barrier_semaphore()
    for present, target in (
        (has_prev, {"section": place - 1}),
        (has_next, {"section": place + 1}),
        (has_low, {"energy": seat - 1}),
        (has_high, {"energy": seat + 1}),
    ):
        @pl.when(present)
        def _():
            pl.semaphore_signal(barrier, inc=1, device_id=target, device_id_type=MESH)

    eye = (
        lax.broadcasted_iota(jnp.int32, (width, width), 0)
        == lax.broadcasted_iota(jnp.int32, (width, width), 1)
    )
    for param in params[:3]:
        param.wait()
    hop = between[0]
    own = jnp.where(eye, onsite[0:1, :], 0.0) + 0.5 * (within[0] + within[0].T)
    hamil[0] = own
    given[0] = hop
    given[1] = own

    def give(index):
        return pltpu.make_async_remote_copy(
            src_ref=sigma.at[0, index], dst_ref=sigma.at[1, index],
            send_sem=send_x.at[index], recv_sem=recv_x.at[index],
            device_id={"section": place - 1}, device_id_type=MESH,
        )

    def give_shared():
        return pltpu.make_async_remote_copy(
            src_ref=given.at[core], dst_ref=given.at[2 + core],
            send_sem=send_g.at[0], recv_sem=recv_g.at[0],
            device_id={"section": place - 1}, device_id_type=MESH,
        )

    def give_partner():
        return pltpu.make_async_remote_copy(
            src_ref=given.at[2 + core], dst_ref=given.at[2 + core],
            send_sem=send_g.at[1], recv_sem=recv_g.at[1],
            device_id=partner, device_id_type=MESH,
        )

    def set_hops(which, value):
        hops[which, 0], hops[which, 1] = split(value)
        hops[which, 2], hops[which, 3] = split(value.T)

    set_hops(0, hop)

    @pl.when(seat == 0)
    def _():
        halo[0:REACH] = jnp.zeros((REACH, 2, width, width), F32)

    @pl.when(seat == spans - 1)
    def _():
        halo[REACH : 2 * REACH] = jnp.zeros((REACH, 2, width, width), F32)

    @pl.when(place == 0)
    def _():
        left[0] = jnp.zeros((width, width), F32)
        left[1] = -CONTACT * matmul((hops[0, 2], hops[0, 3]), (hops[0, 0], hops[0, 1]))

    def set_mats():
        for param in params[3:]:
            param.wait()
        row_group = jnp.broadcast_to(groups[0:1, :].astype(F32), (width, width))
        mat = jnp.where(row_group == row_group.T, coupling[0], 0.0)
        mats[0], mats[1] = split(mat)
        mats[2], mats[3] = split(mat.T)
        outer[...] = mats[...]

        @pl.when(has_prev)
        def _():
            outer[...] = hops[0]


    def inverse(index, which, left_re, left_im):
        number = jnp.full((1, width), 2 * (seat * count + index) + 1, jnp.int32)
        energy = -1.0 + number.astype(F32) / (count * spans)
        sys_re = jnp.where(eye, energy, 0.0) - hamil[which] - sigma[which, index, 0] - left_re
        sys_im = jnp.where(eye, ETA, 0.0) - sigma[which, index, 1] - left_im
        diag_re = jnp.where(eye, sys_re, 0.0)
        diag_im = jnp.where(eye, sys_im, 0.0)
        inverses = []
        for axis in (1, 0):
            real_c = jnp.sum(diag_re, axis=axis, keepdims=True)
            imag_c = jnp.sum(diag_im, axis=axis, keepdims=True)
            modulus = real_c * real_c + imag_c * imag_c
            inverses.append((real_c / modulus, -imag_c / modulus))
        (col_re, col_im), (row_re, row_im) = inverses
        rest_re = jnp.where(eye, 0.0, sys_im * row_im - sys_re * row_re)
        rest_im = jnp.where(eye, 0.0, -(sys_re * row_im + sys_im * row_re))
        square_re, square_im = complex_matmul((rest_re, rest_im), (rest_re, rest_im))
        powers_re, powers_im = complex_matmul(
            (jnp.concatenate([rest_re, square_re], 0), jnp.concatenate([rest_im, square_im], 0)),
            (square_re, square_im),
        )
        sum_re = jnp.where(eye, 1.0, 0.0) + rest_re + square_re + powers_re[:width]
        sum_im = rest_im + square_im + powers_im[:width]
        base_re = col_re * sum_re - col_im * sum_im
        base_im = col_re * sum_im + col_im * sum_re
        out_re, out_im = complex_matmul((base_re, base_im), (powers_re[width:], powers_im[width:]))
        return base_re + out_re, base_im + out_im

    def invert(index):
        local[0, index, 0], local[0, index, 1] = inverse(index, 0, left[0], left[1])

    if paced:
        @pl.when(pacing)
        def _():
            load(order(0)).wait()
            invert(order(0))

    peers = sum(present.astype(jnp.int32) for present in (has_prev, has_next, has_low, has_high))
    pl.semaphore_wait(barrier, peers)

    @pl.when(leaf & has_prev)
    def _():
        give_shared().start()
        for step in range(count):
            index = order(step)
            load(index).wait()
            give(index).start()

    @pl.when(has_prev)
    def _():
        set_mats()

    @pl.when(folding & has_next)
    def _():
        give_shared().wait_recv()
        give_partner().start()
        give_partner().wait_recv()
        set_hops(1, given[2])
        hamil[1] = given[3]

    def forward_copy(which, index, part):
        rows = pl.ds(edges[part], edges[part + 1] - edges[part])
        return pltpu.make_async_remote_copy(
            src_ref=local.at[which, index, :, rows], dst_ref=came_f.at[index, :, rows],
            send_sem=send_f.at[index, part], recv_sem=recv_f.at[index, part],
            device_id={"section": place + 1}, device_id_type=MESH,
        )

    def backward_copy(index, part):
        rows = pl.ds(edges[part], edges[part + 1] - edges[part])
        return pltpu.make_async_remote_copy(
            src_ref=sent_b.at[index, :, rows], dst_ref=came_b.at[index, :, rows],
            send_sem=send_b.at[index, part], recv_sem=recv_b.at[index, part],
            device_id={"section": place - 1}, device_id_type=MESH,
        )

    def halo_up(index):
        slot = index - (count - REACH)
        return pltpu.make_async_remote_copy(
            src_ref=field_y.at[index], dst_ref=halo.at[slot],
            send_sem=send_h.at[slot], recv_sem=recv_h.at[slot],
            device_id={"energy": seat + 1}, device_id_type=MESH,
        )

    def halo_down(index):
        slot = index + REACH
        return pltpu.make_async_remote_copy(
            src_ref=field_y.at[index], dst_ref=halo.at[slot],
            send_sem=send_h.at[slot], recv_sem=recv_h.at[slot],
            device_id={"energy": seat - 1}, device_id_type=MESH,
        )

    def contact(index):
        halves = []
        for part in range(CHUNKS):
            forward_copy(0, index, part).wait_recv()
            rows = slice(edges[part], edges[part + 1])
            field = [split(came_f[index, side, rows]) for side in range(2)]
            half = matmul(join(field, 0), (hops[0, 0], hops[0, 1]))
            size = edges[part + 1] - edges[part]
            halves.append(join([split(half[:size]), split(half[size:])], 1))
        result = matmul((hops[0, 2], hops[0, 3]), join(halves, 0))
        left[0], left[1] = result[:, :width], result[:, width:]

    def launch(index, which):
        for part in range(CHUNKS):
            forward_copy(which, index, part).start()

    def forward(step):
        ahead = step
        if paced:
            ahead = step + pacing.astype(jnp.int32)

            @pl.when(pacing)
            def _():
                @pl.when((step > 0) | odd)
                def _():
                    pl.semaphore_wait(turns, 1)

                launch(order(step), 0)

        @pl.when(ahead < count)
        def _():
            index = order(ahead)
            load(index).wait()

            @pl.when(has_prev)
            def _():
                contact(index)

            invert(index)

            @pl.when(jnp.logical_not(pacing) & (place < fold))
            def _():
                launch(index, 0)

        if paced:
            @pl.when(pacing & ((step < count - 1) | (core == 0)))
            def _():
                forward_copy(0, order(step), CHUNKS - 2).wait_send()
                pl.semaphore_signal(turns, inc=1, device_id=partner, device_id_type=MESH)

    def publish(index):
        return pltpu.make_async_copy(green.at[index], green_out.at[index], keep_g.at[index])

    def publish_field(index):
        return pltpu.make_async_copy(field_y.at[index], fields_out.at[index + REACH], keep_y.at[index])

    def publish_halo(slot):
        target = slot if slot < REACH else slot + count
        return pltpu.make_async_copy(halo.at[slot], fields_out.at[target], keep_h.at[slot])

    def neighbours(index):
        publish_field(index).start()

        @pl.when(has_high & (index >= count - REACH))
        def _():
            halo_up(index).start()

        @pl.when(has_low & (index < REACH))
        def _():
            halo_down(index).start()

    def finish(index):
        field = join([split(green[index, 0, side]) for side in range(2)], 0)
        half = matmul(field, (mats[2], mats[3]))
        half = join([split(half[:width]), split(half[width:])], 1)
        result = matmul((mats[0], mats[1]), half)
        field_y[index, 0] = result[:, :width]
        field_y[index, 1] = result[:, width:]
        neighbours(index)

    def send_back(index, out_re, out_im):
        sent_b[index, 0] = out_re
        sent_b[index, 1] = out_im
        for part in range(CHUNKS):
            backward_copy(index, part).start()

    def prepare(index):
        base = [split(local[0, index, side]) for side in range(2)]
        lefts = matmul((outer[0], outer[1]), join(base, 1))
        rights = matmul(join(base, 0), (outer[2], outer[3]))
        lefts = splits(lefts[:, :width], lefts[:, width:])
        ready_r[0], ready_r[1] = complex_columns(splits(rights[:width], rights[width:]))
        ready_w[...] = matmul(join(lefts, 0), (outer[2], outer[3]))
        ready_l[0], ready_l[1] = complex_rows(lefts)

    def backward(index):
        columns = ready_r[0], ready_r[1]
        mids = []
        for part in range(CHUNKS):
            backward_copy(index, part).wait_recv()
            rows = slice(edges[part], edges[part + 1])
            incoming = join([split(came_b[index, side, rows]) for side in range(2)], 1)
            mids.append(matmul(incoming, columns))
        mid = jnp.concatenate(mids, axis=0)
        out = matmul((ready_l[0], ready_l[1]), complex_columns(splits(mid[:, :width], mid[:, width:])))
        out_re, out_im = ready_w[:width] + out[:, :width], ready_w[width:] + out[:, width:]

        @pl.when(has_prev)
        def _():
            send_back(index, out_re, out_im)

        @pl.when(jnp.logical_not(has_prev))
        def _():
            field_y[index, 0] = out_re
            field_y[index, 1] = out_im
            neighbours(index)

        base_re, base_im = local[0, index, 0], local[0, index, 1]
        mid = complex_matmul((came_b[index, 0], came_b[index, 1]), (base_re, base_im))
        out_re, out_im = complex_matmul((base_re, base_im), mid)
        green[index, 0, 0] = base_re + out_re
        green[index, 0, 1] = base_im + out_im
        publish(index).start()

        @pl.when(has_prev)
        def _():
            finish(index)

    def refold(index):
        give(index).wait_recv()
        base_re, base_im = local[0, index, 0], local[0, index, 1]
        base = splits(base_re, base_im)
        half = matmul(join(base, 0), (hops[1, 0], hops[1, 1]))
        half_re, half_im = half[:width], half[width:]
        half = join(splits(half_re, half_im), 1)
        result = matmul((hops[1, 2], hops[1, 3]), half)
        end_re, end_im = inverse(index, 1, result[:, :width], result[:, width:])
        outer_l = matmul((hops[0, 0], hops[0, 1]), half)
        inner_r = matmul((hops[1, 2], hops[1, 3]), join(base, 1))
        inner_re, inner_im = inner_r[:, :width], inner_r[:, width:]
        outer_r = matmul(join(splits(inner_re, inner_im), 0), (hops[0, 2], hops[0, 3]))
        whole = matmul((hops[0, 0], hops[0, 1]), join(base, 1))
        whole = join(splits(whole[:, :width], whole[:, width:]), 0)
        whole = matmul(whole, (hops[0, 2], hops[0, 3]))
        mid = complex_matmul((end_re, end_im), (outer_r[:width], outer_r[width:]))
        out_re, out_im = complex_matmul((outer_l[:, :width], outer_l[:, width:]), mid)
        local[1, index, 0], local[1, index, 1] = end_re, end_im

        @pl.when(has_prev)
        def _():
            send_back(index, whole[:width] + out_re, whole[width:] + out_im)

        launch(index, 1)
        mid = complex_matmul((local[1, index, 0], local[1, index, 1]), (inner_re, inner_im))
        out_re, out_im = complex_matmul((half_re, half_im), mid)
        green[index, 0, 0] = local[0, index, 0] + out_re
        green[index, 0, 1] = local[0, index, 1] + out_im
        publish(index).start()
        finish(index)

    def receive(index):
        for part in range(CHUNKS):
            forward_copy(0, index, part).wait_recv()
        green[index, 0] = came_f[index]
        publish(index).start()
        finish(index)

    behind = 2 * (fold - place)

    def turn(step, carry):
        @pl.when((place <= fold) & (step < count))
        def _():
            forward(step)

        @pl.when((step == 0) & jnp.logical_not(has_prev))
        def _():
            set_mats()

        @pl.when((place < fold) & (step >= behind) & (step < behind + count))
        def _():
            backward(order(step - behind))

        @pl.when((place < fold) & (step + 1 >= behind) & (step + 1 < behind + count))
        def _():
            prepare(order(step + 1 - behind))

        @pl.when(folding & has_next & (step < count))
        def _():
            refold(order(step))

        @pl.when(leaf & has_prev & (step < count))
        def _():
            receive(order(step))

        return carry

    lax.fori_loop(0, count + 2 * fold, turn, 0)

    @pl.when(has_low)
    def _():
        for slot in range(REACH):
            halo_up(count - REACH + slot).wait_recv()

    for slot in range(REACH):
        publish_halo(slot).start()

    @pl.when(has_high)
    def _():
        for slot in range(REACH):
            halo_down(slot).wait_recv()

    for slot in range(REACH):
        publish_halo(REACH + slot).start()

    @pl.when(has_next)
    def _():
        for step in range(count):
            for part in range(CHUNKS):
                if paced and part == CHUNKS - 2:
                    waited = pacing & ((step < count - 1) | (core == 0))

                    @pl.when(jnp.logical_not(waited))
                    def _():
                        forward_copy(0, order(step), part).wait_send()
                else:
                    forward_copy(0, order(step), part).wait_send()

    @pl.when(has_prev & (place < last))
    def _():
        for index in range(count):
            for part in range(CHUNKS):
                backward_copy(index, part).wait_send()

    @pl.when(leaf & has_prev)
    def _():
        give_shared().wait_send()
        for index in range(count):
            give(index).wait_send()

    @pl.when(folding & has_next)
    def _():
        give_partner().wait_send()

    @pl.when(has_high)
    def _():
        for slot in range(REACH):
            halo_up(count - REACH + slot).wait_send()

    @pl.when(has_low)
    def _():
        for slot in range(REACH):
            halo_down(slot).wait_send()

    for index in range(count):
        publish(index).wait()
        publish_field(index).wait()
    for slot in range(2 * REACH):
        publish_halo(slot).wait()


def combine(offsets, strength, green, fields, green_out, self_out, held, block, total, load_g, load_f, save_g, save_s):
    count = green.shape[0]
    loads = [
        pltpu.make_async_copy(fields.at[slot], block.at[slot], load_f.at[slot])
        for slot in range(count + 2 * REACH)
    ]
    brings = [pltpu.make_async_copy(green.at[index], held.at[index], load_g.at[index]) for index in range(count)]
    keeps = [pltpu.make_async_copy(held.at[index], green_out.at[index], save_g.at[index]) for index in range(count)]
    saves = [pltpu.make_async_copy(total.at[index], self_out.at[index], save_s.at[index]) for index in range(count)]
    for copy in brings + loads:
        copy.start()
    near = jnp.float32(0.0)
    far = jnp.float32(0.0)
    for mode in range(offsets.shape[0]):
        near = near + jnp.where(offsets[mode] == 1, strength[mode], 0.0)
        far = far + jnp.where(offsets[mode] == 2, strength[mode], 0.0)
    for bring, keep in zip(brings, keeps):
        bring.wait()
        keep.start()
    arrived = 0
    for index in range(count):
        while arrived <= index + 2 * REACH:
            loads[arrived].wait()
            arrived += 1
        middle = index + REACH
        total[index, 0] = near * (block[middle - 1] + block[middle + 1]) + far * (
            block[middle - 2] + block[middle + 2]
        )
        saves[index].start()
    for copy in keeps + saves:
        copy.wait()


def per_device(self_in, onsite, within, between, coupling, groups, offsets, strength):
    count, width = self_in.shape[0], self_in.shape[3]
    smem = pl.BlockSpec(memory_space=pltpu.SMEM)
    hbm = pl.BlockSpec(memory_space=pltpu.HBM)
    shape = jax.ShapeDtypeStruct(self_in.shape, F32)
    dma = pltpu.SemaphoreType.DMA
    blocks = pltpu.VMEM((count, 2, width, width), F32)
    fields = jax.ShapeDtypeStruct((count + 2 * REACH, 2, width, width), F32)
    green, fields = pl.pallas_call(
        kernel,
        out_shape=(shape, fields),
        in_specs=[hbm] * 6,
        out_specs=(hbm, hbm),
        scratch_shapes=[
            pltpu.VMEM(self_in.shape, F32),
            dma((count,)), dma((count,)), dma((2 * REACH,)),
            pltpu.VMEM(onsite.shape, F32),
            pltpu.VMEM(within.shape, F32),
            pltpu.VMEM(between.shape, F32),
            pltpu.VMEM(coupling.shape, F32),
            pltpu.VMEM(groups.shape, jnp.int32),
            dma((5,)),
            pltpu.VMEM((2, width, 2 * width), BF16),
            pltpu.VMEM((2, 2 * width, 2 * width), BF16),
            pltpu.VMEM((2 * width, width), F32),
            pltpu.VMEM((2, width, width), F32),
            pltpu.VMEM((2, 4, width, width), BF16),
            pltpu.VMEM((4, width, width), BF16),
            pltpu.VMEM((4, width, width), BF16),
            pltpu.VMEM((2, width, width), F32),
            pltpu.VMEM((2, count, 2, width, width), F32),
            pltpu.VMEM((2, count, 2, width, width), F32),
            blocks, blocks, blocks,
            pltpu.VMEM((4, width, width), F32),
            blocks,
            pltpu.VMEM((2 * REACH, 2, width, width), F32),
            dma((count,)),
            dma((count, CHUNKS)), dma((count, CHUNKS)), dma((count, CHUNKS)), dma((count, CHUNKS)),
            dma((2 * REACH,)), dma((2 * REACH,)),
            dma((count,)), dma((count,)), dma((2,)), dma((2,)),
            pltpu.SemaphoreType.REGULAR,
        ],
        compiler_params=pltpu.CompilerParams(
            collective_id=0, has_side_effects=True, vmem_limit_bytes=60 * 2**20
        ),
    )(self_in, onsite, within, between, coupling, groups)
    return pl.pallas_call(
        combine,
        out_shape=(shape, shape),
        in_specs=[smem] * 2 + [hbm] * 2,
        out_specs=(hbm, hbm),
        scratch_shapes=[
            pltpu.VMEM(self_in.shape, F32),
            pltpu.VMEM((count + 2 * REACH, 2, width, width), F32),
            pltpu.VMEM(self_in.shape, F32),
            dma((count,)), dma((count + 2 * REACH,)), dma((count,)), dma((count,)),
        ],
        compiler_params=pltpu.CompilerParams(vmem_limit_bytes=60 * 2**20),
    )(offsets, strength, green, fields)


def solution(mesh):
    placed = (
        P("energy", "section", None, None, None),
        P("section", None),
        P("section", None, None),
        P("section", None, None),
        P("section", None, None),
        P("section", None),
        P(),
        P(),
    )
    return jax.shard_map(
        per_device,
        mesh=mesh,
        in_specs=placed,
        out_specs=(
            P("energy", "section", None, None, None),
            P("energy", "section", None, None, None),
        ),
        check_vma=False,
    )
```

```python
import jax
import jax.numpy as jnp
from jax import lax
from jax.experimental import pallas as pl
from jax.experimental.pallas import tpu as pltpu
from jax.sharding import PartitionSpec as P

ETA = 1.0
CONTACT = 0.6
REACH = 2
CHUNKS = 2

F32 = jnp.float32
BF16 = jnp.bfloat16
MESH = pl.DeviceIdType.MESH


def split(value):
    high = value.astype(BF16)
    return high, (value - high.astype(F32)).astype(BF16)


def join(pieces, axis):
    return tuple(jnp.concatenate(parts, axis=axis) for parts in zip(*pieces))


def dot(left, right):
    return jnp.dot(left, right, preferred_element_type=F32)


def matmul(left, right):
    (left_h, left_l), (right_h, right_l) = left, right
    return dot(left_h, right_h) + (dot(left_h, right_l) + dot(left_l, right_h))


def minus(pair):
    return tuple(-part for part in pair)


def complex_columns(block):
    return join([join([block[0], block[1]], 1), join([minus(block[1]), block[0]], 1)], 0)


def complex_rows(block):
    return join(block, 1)


def splits(real, imag):
    return split(real), split(imag)


def complex_matmul(left, right):
    first = matmul(split(left[0]), split(right[0]))
    second = matmul(split(left[1]), split(right[1]))
    third = matmul(split(left[0] + left[1]), split(right[0] + right[1]))
    return first - second, third - first - second


def kernel(
    offsets, strength, self_in, onsite_in, within_in, between_in, coupling_in, groups_in,
    green_out, total_out,
    green, total, keep_g, keep_t,
    onsite, within, between, coupling, groups, load_p,
    ready_l, ready_r, ready_w, hamil, hops, mats, outer, left, sigma, local, came_f, came_b, sent_b, given, field_y, halo,
    load_s, send_f, recv_f, send_b, recv_b, send_h, recv_h, send_x, recv_x, send_g, recv_g,
    turns,
):
    count, width = self_in.shape[0], self_in.shape[3]
    sections, place = lax.axis_size("section"), lax.axis_index("section")
    spans, seat = lax.axis_size("energy"), lax.axis_index("energy")
    last = sections - 1
    fold = max(sections - 2, 0)
    has_prev, has_next = place > 0, place < last
    has_low, has_high = seat > 0, seat < spans - 1
    folding, leaf = place == fold, place == last
    edges = (0, width * 13 // 16 // 16 * 16, width)
    spans_of = tuple(zip(edges[:-1], edges[1:]))
    core = lax.rem(seat, 2)
    odd = core == 1
    partner = {"energy": seat + 1 - 2 * core}
    paced = sections > 2
    pacing = (place == 0) if paced else (place < 0)

    def order(step):
        return jnp.where(odd, count - 1 - step, step)

    def load(index):
        return pltpu.make_async_copy(self_in.at[index, 0], sigma.at[0, index], load_s.at[index])

    params = [
        pltpu.make_async_copy(source, target, load_p.at[number])
        for number, (source, target) in enumerate(
            (
                (between_in, between), (within_in, within), (onsite_in, onsite),
                (groups_in, groups), (coupling_in, coupling),
            )
        )
    ]
    for param in params[:3]:
        param.start()
    for step in range(count):
        load(order(step)).start()
    for param in params[3:]:
        param.start()

    barrier = pltpu.get_barrier_semaphore()
    for present, target in (
        (has_prev, {"section": place - 1}),
        (has_next, {"section": place + 1}),
        (has_low, {"energy": seat - 1}),
        (has_high, {"energy": seat + 1}),
    ):
        @pl.when(present)
        def _():
            pl.semaphore_signal(barrier, inc=1, device_id=target, device_id_type=MESH)

    eye = (
        lax.broadcasted_iota(jnp.int32, (width, width), 0)
        == lax.broadcasted_iota(jnp.int32, (width, width), 1)
    )
    for param in params[:3]:
        param.wait()
    hop = between[0]
    own = jnp.where(eye, onsite[0:1, :], 0.0) + 0.5 * (within[0] + within[0].T)
    hamil[0] = own
    given[0] = hop
    given[1] = own

    def give(index):
        return pltpu.make_async_remote_copy(
            src_ref=sigma.at[0, index], dst_ref=sigma.at[1, index],
            send_sem=send_x.at[index], recv_sem=recv_x.at[index],
            device_id={"section": place - 1}, device_id_type=MESH,
        )

    def give_shared():
        return pltpu.make_async_remote_copy(
            src_ref=given.at[core], dst_ref=given.at[2 + core],
            send_sem=send_g.at[0], recv_sem=recv_g.at[0],
            device_id={"section": place - 1}, device_id_type=MESH,
        )

    def give_partner():
        return pltpu.make_async_remote_copy(
            src_ref=given.at[2 + core], dst_ref=given.at[2 + core],
            send_sem=send_g.at[1], recv_sem=recv_g.at[1],
            device_id=partner, device_id_type=MESH,
        )

    def set_hops(which, value):
        hops[which, 0], hops[which, 1] = split(value)
        hops[which, 2], hops[which, 3] = split(value.T)

    set_hops(0, hop)

    @pl.when(seat == 0)
    def _():
        halo[0:REACH] = jnp.zeros((REACH, 2, width, width), F32)

    @pl.when(seat == spans - 1)
    def _():
        halo[REACH : 2 * REACH] = jnp.zeros((REACH, 2, width, width), F32)

    @pl.when(place == 0)
    def _():
        left[0] = jnp.zeros((width, width), F32)
        left[1] = -CONTACT * matmul((hops[0, 2], hops[0, 3]), (hops[0, 0], hops[0, 1]))

    def set_mats():
        for param in params[3:]:
            param.wait()
        row_group = jnp.broadcast_to(groups[0:1, :].astype(F32), (width, width))
        mat = jnp.where(row_group == row_group.T, coupling[0], 0.0)
        mats[0], mats[1] = split(mat)
        mats[2], mats[3] = split(mat.T)
        outer[...] = mats[...]

        @pl.when(has_prev)
        def _():
            outer[...] = hops[0]


    def inverse(index, which, left_re, left_im):
        number = jnp.full((1, width), 2 * (seat * count + index) + 1, jnp.int32)
        energy = -1.0 + number.astype(F32) / (count * spans)
        sys_re = jnp.where(eye, energy, 0.0) - hamil[which] - sigma[which, index, 0] - left_re
        sys_im = jnp.where(eye, ETA, 0.0) - sigma[which, index, 1] - left_im
        diag_re = jnp.where(eye, sys_re, 0.0)
        diag_im = jnp.where(eye, sys_im, 0.0)
        inverses = []
        for axis in (1, 0):
            real_c = jnp.sum(diag_re, axis=axis, keepdims=True)
            imag_c = jnp.sum(diag_im, axis=axis, keepdims=True)
            modulus = real_c * real_c + imag_c * imag_c
            inverses.append((real_c / modulus, -imag_c / modulus))
        (col_re, col_im), (row_re, row_im) = inverses
        rest_re = jnp.where(eye, 0.0, sys_im * row_im - sys_re * row_re)
        rest_im = jnp.where(eye, 0.0, -(sys_re * row_im + sys_im * row_re))
        square_re, square_im = complex_matmul((rest_re, rest_im), (rest_re, rest_im))
        powers_re, powers_im = complex_matmul(
            (jnp.concatenate([rest_re, square_re], 0), jnp.concatenate([rest_im, square_im], 0)),
            (square_re, square_im),
        )
        sum_re = jnp.where(eye, 1.0, 0.0) + rest_re + square_re + powers_re[:width]
        sum_im = rest_im + square_im + powers_im[:width]
        base_re = col_re * sum_re - col_im * sum_im
        base_im = col_re * sum_im + col_im * sum_re
        out_re, out_im = complex_matmul((base_re, base_im), (powers_re[width:], powers_im[width:]))
        return base_re + out_re, base_im + out_im

    def invert(index):
        local[0, index, 0], local[0, index, 1] = inverse(index, 0, left[0], left[1])

    if paced:
        @pl.when(pacing)
        def _():
            load(order(0)).wait()
            invert(order(0))

    peers = sum(present.astype(jnp.int32) for present in (has_prev, has_next, has_low, has_high))
    pl.semaphore_wait(barrier, peers)

    @pl.when(leaf & has_prev)
    def _():
        give_shared().start()
        for step in range(count):
            index = order(step)
            load(index).wait()
            give(index).start()

    @pl.when(has_prev)
    def _():
        set_mats()

    @pl.when(folding & has_next)
    def _():
        give_shared().wait_recv()
        give_partner().start()
        give_partner().wait_recv()
        set_hops(1, given[2])
        hamil[1] = given[3]

    def forward_copy(which, index, part):
        rows = pl.ds(edges[part], edges[part + 1] - edges[part])
        return pltpu.make_async_remote_copy(
            src_ref=local.at[which, index, :, rows], dst_ref=came_f.at[index, :, rows],
            send_sem=send_f.at[index, part], recv_sem=recv_f.at[index, part],
            device_id={"section": place + 1}, device_id_type=MESH,
        )

    def backward_copy(index, part):
        rows = pl.ds(edges[part], edges[part + 1] - edges[part])
        return pltpu.make_async_remote_copy(
            src_ref=sent_b.at[index, :, rows], dst_ref=came_b.at[index, :, rows],
            send_sem=send_b.at[index, part], recv_sem=recv_b.at[index, part],
            device_id={"section": place - 1}, device_id_type=MESH,
        )

    def halo_up(index):
        slot = index - (count - REACH)
        return pltpu.make_async_remote_copy(
            src_ref=field_y.at[index], dst_ref=halo.at[slot],
            send_sem=send_h.at[slot], recv_sem=recv_h.at[slot],
            device_id={"energy": seat + 1}, device_id_type=MESH,
        )

    def halo_down(index):
        slot = index + REACH
        return pltpu.make_async_remote_copy(
            src_ref=field_y.at[index], dst_ref=halo.at[slot],
            send_sem=send_h.at[slot], recv_sem=recv_h.at[slot],
            device_id={"energy": seat - 1}, device_id_type=MESH,
        )

    def contact(index):
        halves = []
        for part in range(CHUNKS):
            forward_copy(0, index, part).wait_recv()
            rows = slice(edges[part], edges[part + 1])
            field = [split(came_f[index, side, rows]) for side in range(2)]
            half = matmul(join(field, 0), (hops[0, 0], hops[0, 1]))
            size = edges[part + 1] - edges[part]
            halves.append(join([split(half[:size]), split(half[size:])], 1))
        result = matmul((hops[0, 2], hops[0, 3]), join(halves, 0))
        left[0], left[1] = result[:, :width], result[:, width:]

    def launch(index, which):
        for part in range(CHUNKS):
            forward_copy(which, index, part).start()

    def forward(step):
        ahead = step
        if paced:
            ahead = step + pacing.astype(jnp.int32)

            @pl.when(pacing)
            def _():
                @pl.when((step > 0) | odd)
                def _():
                    pl.semaphore_wait(turns, 1)

                launch(order(step), 0)

        @pl.when(ahead < count)
        def _():
            index = order(ahead)
            load(index).wait()

            @pl.when(has_prev)
            def _():
                contact(index)

            invert(index)

            @pl.when(jnp.logical_not(pacing) & (place < fold))
            def _():
                launch(index, 0)

        if paced:
            @pl.when(pacing & ((step < count - 1) | (core == 0)))
            def _():
                forward_copy(0, order(step), CHUNKS - 2).wait_send()
                pl.semaphore_signal(turns, inc=1, device_id=partner, device_id_type=MESH)

    def publish(index):
        return pltpu.make_async_copy(green.at[index], green_out.at[index], keep_g.at[index])

    def publish_total(index):
        return pltpu.make_async_copy(total.at[index], total_out.at[index], keep_t.at[index])

    def neighbours(index):
        @pl.when(has_high & (index >= count - REACH))
        def _():
            halo_up(index).start()

        @pl.when(has_low & (index < REACH))
        def _():
            halo_down(index).start()

    def finish(index):
        field = join([split(green[index, 0, side]) for side in range(2)], 0)
        half = matmul(field, (mats[2], mats[3]))
        half = join([split(half[:width]), split(half[width:])], 1)
        result = matmul((mats[0], mats[1]), half)
        field_y[index, 0] = result[:, :width]
        field_y[index, 1] = result[:, width:]
        neighbours(index)

    def send_back(index, out_re, out_im):
        sent_b[index, 0] = out_re
        sent_b[index, 1] = out_im
        for part in range(CHUNKS):
            backward_copy(index, part).start()

    def prepare(index):
        base = [split(local[0, index, side]) for side in range(2)]
        lefts = matmul((outer[0], outer[1]), join(base, 1))
        rights = matmul(join(base, 0), (outer[2], outer[3]))
        lefts = splits(lefts[:, :width], lefts[:, width:])
        ready_r[0], ready_r[1] = complex_columns(splits(rights[:width], rights[width:]))
        ready_w[...] = matmul(join(lefts, 0), (outer[2], outer[3]))
        ready_l[0], ready_l[1] = complex_rows(lefts)

    def backward(index):
        columns = ready_r[0], ready_r[1]
        mids = []
        for part in range(CHUNKS):
            backward_copy(index, part).wait_recv()
            rows = slice(edges[part], edges[part + 1])
            incoming = join([split(came_b[index, side, rows]) for side in range(2)], 1)
            mids.append(matmul(incoming, columns))
        mid = jnp.concatenate(mids, axis=0)
        out = matmul((ready_l[0], ready_l[1]), complex_columns(splits(mid[:, :width], mid[:, width:])))
        out_re, out_im = ready_w[:width] + out[:, :width], ready_w[width:] + out[:, width:]

        @pl.when(has_prev)
        def _():
            send_back(index, out_re, out_im)

        @pl.when(jnp.logical_not(has_prev))
        def _():
            field_y[index, 0] = out_re
            field_y[index, 1] = out_im
            neighbours(index)

        base_re, base_im = local[0, index, 0], local[0, index, 1]
        mid = complex_matmul((came_b[index, 0], came_b[index, 1]), (base_re, base_im))
        out_re, out_im = complex_matmul((base_re, base_im), mid)
        green[index, 0, 0] = base_re + out_re
        green[index, 0, 1] = base_im + out_im
        publish(index).start()

        @pl.when(has_prev)
        def _():
            finish(index)

    def refold(index):
        give(index).wait_recv()
        base_re, base_im = local[0, index, 0], local[0, index, 1]
        base = splits(base_re, base_im)
        half = matmul(join(base, 0), (hops[1, 0], hops[1, 1]))
        half_re, half_im = half[:width], half[width:]
        half = join(splits(half_re, half_im), 1)
        result = matmul((hops[1, 2], hops[1, 3]), half)
        end_re, end_im = inverse(index, 1, result[:, :width], result[:, width:])
        outer_l = matmul((hops[0, 0], hops[0, 1]), half)
        inner_r = matmul((hops[1, 2], hops[1, 3]), join(base, 1))
        inner_re, inner_im = inner_r[:, :width], inner_r[:, width:]
        outer_r = matmul(join(splits(inner_re, inner_im), 0), (hops[0, 2], hops[0, 3]))
        whole = matmul((hops[0, 0], hops[0, 1]), join(base, 1))
        whole = join(splits(whole[:, :width], whole[:, width:]), 0)
        whole = matmul(whole, (hops[0, 2], hops[0, 3]))
        mid = complex_matmul((end_re, end_im), (outer_r[:width], outer_r[width:]))
        out_re, out_im = complex_matmul((outer_l[:, :width], outer_l[:, width:]), mid)
        local[1, index, 0], local[1, index, 1] = end_re, end_im

        @pl.when(has_prev)
        def _():
            send_back(index, whole[:width] + out_re, whole[width:] + out_im)

        launch(index, 1)
        mid = complex_matmul((local[1, index, 0], local[1, index, 1]), (inner_re, inner_im))
        out_re, out_im = complex_matmul((half_re, half_im), mid)
        green[index, 0, 0] = local[0, index, 0] + out_re
        green[index, 0, 1] = local[0, index, 1] + out_im
        publish(index).start()
        finish(index)

    def receive(index):
        for part in range(CHUNKS):
            forward_copy(0, index, part).wait_recv()
        green[index, 0] = came_f[index]
        publish(index).start()
        finish(index)

    behind = 2 * (fold - place)

    def turn(step, carry):
        @pl.when((place <= fold) & (step < count))
        def _():
            forward(step)

        @pl.when((step == 0) & jnp.logical_not(has_prev))
        def _():
            set_mats()

        @pl.when((place < fold) & (step >= behind) & (step < behind + count))
        def _():
            backward(order(step - behind))

        @pl.when((place < fold) & (step + 1 >= behind) & (step + 1 < behind + count))
        def _():
            prepare(order(step + 1 - behind))

        @pl.when(folding & has_next & (step < count))
        def _():
            refold(order(step))

        @pl.when(leaf & has_prev & (step < count))
        def _():
            receive(order(step))

        return carry

    lax.fori_loop(0, count + 2 * fold, turn, 0)

    near = jnp.float32(0.0)
    far = jnp.float32(0.0)
    for mode in range(offsets.shape[0]):
        near = near + jnp.where(offsets[mode] == 1, strength[mode], 0.0)
        far = far + jnp.where(offsets[mode] == 2, strength[mode], 0.0)

    def block(index, side):
        if index < 0:
            return halo[index + REACH, side]
        if index >= count:
            return halo[index - count + REACH, side]
        return field_y[index, side]

    @pl.when(has_low)
    def _():
        for slot in range(REACH):
            halo_up(count - REACH + slot).wait_recv()

    for index in range(count):
        if index == max(count - REACH, 0):
            @pl.when(has_high)
            def _():
                for slot in range(REACH):
                    halo_down(slot).wait_recv()

        for side in range(2):
            total[index, 0, side] = near * (
                block(index - 1, side) + block(index + 1, side)
            ) + far * (block(index - 2, side) + block(index + 2, side))
        publish_total(index).start()

    @pl.when(has_next)
    def _():
        for step in range(count):
            for part in range(CHUNKS):
                if paced and part == CHUNKS - 2:
                    waited = pacing & ((step < count - 1) | (core == 0))

                    @pl.when(jnp.logical_not(waited))
                    def _():
                        forward_copy(0, order(step), part).wait_send()
                else:
                    forward_copy(0, order(step), part).wait_send()

    @pl.when(has_prev & (place < last))
    def _():
        for index in range(count):
            for part in range(CHUNKS):
                backward_copy(index, part).wait_send()

    @pl.when(leaf & has_prev)
    def _():
        give_shared().wait_send()
        for index in range(count):
            give(index).wait_send()

    @pl.when(folding & has_next)
    def _():
        give_partner().wait_send()

    @pl.when(has_high)
    def _():
        for slot in range(REACH):
            halo_up(count - REACH + slot).wait_send()

    @pl.when(has_low)
    def _():
        for slot in range(REACH):
            halo_down(slot).wait_send()

    for index in range(count):
        publish(index).wait()
        publish_total(index).wait()


def deliver(green, total, green_out, self_out, held, load, save):
    count = green.shape[0]
    loads, saves = [], []
    for side, (source, target) in enumerate(((green, green_out), (total, self_out))):
        for index in range(count):
            slot = side * count + index
            loads.append(pltpu.make_async_copy(source.at[index], held.at[slot], load.at[slot]))
            saves.append(pltpu.make_async_copy(held.at[slot], target.at[index], save.at[slot]))
    for copy in loads:
        copy.start()
    for arrival, departure in zip(loads, saves):
        arrival.wait()
        departure.start()
    for copy in saves:
        copy.wait()


def per_device(self_in, onsite, within, between, coupling, groups, offsets, strength):
    count, width = self_in.shape[0], self_in.shape[3]
    smem = pl.BlockSpec(memory_space=pltpu.SMEM)
    hbm = pl.BlockSpec(memory_space=pltpu.HBM)
    shape = jax.ShapeDtypeStruct(self_in.shape, F32)
    dma = pltpu.SemaphoreType.DMA
    blocks = pltpu.VMEM((count, 2, width, width), F32)
    green, total = pl.pallas_call(
        kernel,
        out_shape=(shape, shape),
        in_specs=[smem] * 2 + [hbm] * 6,
        out_specs=(hbm, hbm),
        scratch_shapes=[
            pltpu.VMEM(self_in.shape, F32),
            pltpu.VMEM(self_in.shape, F32),
            dma((count,)), dma((count,)),
            pltpu.VMEM(onsite.shape, F32),
            pltpu.VMEM(within.shape, F32),
            pltpu.VMEM(between.shape, F32),
            pltpu.VMEM(coupling.shape, F32),
            pltpu.VMEM(groups.shape, jnp.int32),
            dma((5,)),
            pltpu.VMEM((2, width, 2 * width), BF16),
            pltpu.VMEM((2, 2 * width, 2 * width), BF16),
            pltpu.VMEM((2 * width, width), F32),
            pltpu.VMEM((2, width, width), F32),
            pltpu.VMEM((2, 4, width, width), BF16),
            pltpu.VMEM((4, width, width), BF16),
            pltpu.VMEM((4, width, width), BF16),
            pltpu.VMEM((2, width, width), F32),
            pltpu.VMEM((2, count, 2, width, width), F32),
            pltpu.VMEM((2, count, 2, width, width), F32),
            blocks, blocks, blocks,
            pltpu.VMEM((4, width, width), F32),
            blocks,
            pltpu.VMEM((2 * REACH, 2, width, width), F32),
            dma((count,)),
            dma((count, CHUNKS)), dma((count, CHUNKS)), dma((count, CHUNKS)), dma((count, CHUNKS)),
            dma((2 * REACH,)), dma((2 * REACH,)),
            dma((count,)), dma((count,)), dma((2,)), dma((2,)),
            pltpu.SemaphoreType.REGULAR,
        ],
        compiler_params=pltpu.CompilerParams(
            collective_id=0, has_side_effects=True, vmem_limit_bytes=60 * 2**20
        ),
    )(offsets, strength, self_in, onsite, within, between, coupling, groups)
    return pl.pallas_call(
        deliver,
        out_shape=(shape, shape),
        in_specs=[hbm] * 2,
        out_specs=(hbm, hbm),
        scratch_shapes=[
            pltpu.VMEM((2 * count,) + self_in.shape[1:], F32),
            dma((2 * count,)), dma((2 * count,)),
        ],
        compiler_params=pltpu.CompilerParams(vmem_limit_bytes=60 * 2**20),
    )(green, total)


def solution(mesh):
    placed = (
        P("energy", "section", None, None, None),
        P("section", None),
        P("section", None, None),
        P("section", None, None),
        P("section", None, None),
        P("section", None),
        P(),
        P(),
    )
    return jax.shard_map(
        per_device,
        mesh=mesh,
        in_specs=placed,
        out_specs=(
            P("energy", "section", None, None, None),
            P("energy", "section", None, None, None),
        ),
        check_vma=False,
    )
```

```python
import jax
import jax.numpy as jnp
from jax import lax
from jax.experimental import pallas as pl
from jax.experimental.pallas import tpu as pltpu
from jax.sharding import PartitionSpec as P

ETA = 1.0
CONTACT = 0.6
REACH = 2
CHUNKS = 2

F32 = jnp.float32
BF16 = jnp.bfloat16
MESH = pl.DeviceIdType.MESH


def split(value):
    high = value.astype(BF16)
    return high, (value - high.astype(F32)).astype(BF16)


def join(pieces, axis):
    return tuple(jnp.concatenate(parts, axis=axis) for parts in zip(*pieces))


def dot(left, right):
    return jnp.dot(left, right, preferred_element_type=F32)


def matmul(left, right):
    (left_h, left_l), (right_h, right_l) = left, right
    return dot(left_h, right_h) + (dot(left_h, right_l) + dot(left_l, right_h))


def minus(pair):
    return tuple(-part for part in pair)


def complex_columns(block):
    return join([join([block[0], block[1]], 1), join([minus(block[1]), block[0]], 1)], 0)


def complex_rows(block):
    return join(block, 1)


def splits(real, imag):
    return split(real), split(imag)


def complex_matmul(left, right):
    first = matmul(split(left[0]), split(right[0]))
    second = matmul(split(left[1]), split(right[1]))
    third = matmul(split(left[0] + left[1]), split(right[0] + right[1]))
    return first - second, third - first - second


def kernel(
    offsets, strength, self_in, onsite_in, within_in, between_in, coupling_in, groups_in,
    green_out, total_out,
    green, total, keep_g, keep_t,
    onsite, within, between, coupling, groups, load_p,
    ready_l, ready_r, ready_w, hamil, hops, mats, outer, left, sigma, local, came_f, came_b, sent_b, given, field_y, halo,
    load_s, send_f, recv_f, send_b, recv_b, send_h, recv_h, send_x, recv_x, send_g, recv_g,
    turns,
):
    count, width = self_in.shape[0], self_in.shape[3]
    sections, place = lax.axis_size("section"), lax.axis_index("section")
    spans, seat = lax.axis_size("energy"), lax.axis_index("energy")
    last = sections - 1
    fold = max(sections - 2, 0)
    has_prev, has_next = place > 0, place < last
    has_low, has_high = seat > 0, seat < spans - 1
    folding, leaf = place == fold, place == last
    edges = (0, width * 13 // 16 // 16 * 16, width)
    spans_of = tuple(zip(edges[:-1], edges[1:]))
    core = lax.rem(seat, 2)
    odd = core == 1
    partner = {"energy": seat + 1 - 2 * core}
    paced = sections > 2
    pacing = (place == 0) if paced else (place < 0)

    def order(step):
        return jnp.where(odd, count - 1 - step, step)

    def load(index):
        return pltpu.make_async_copy(self_in.at[index, 0], sigma.at[0, index], load_s.at[index])

    params = [
        pltpu.make_async_copy(source, target, load_p.at[number])
        for number, (source, target) in enumerate(
            (
                (between_in, between), (within_in, within), (onsite_in, onsite),
                (groups_in, groups), (coupling_in, coupling),
            )
        )
    ]
    for param in params[:3]:
        param.start()
    for step in range(count):
        load(order(step)).start()
    for param in params[3:]:
        param.start()

    barrier = pltpu.get_barrier_semaphore()
    for present, target in (
        (has_prev, {"section": place - 1}),
        (has_next, {"section": place + 1}),
        (has_low, {"energy": seat - 1}),
        (has_high, {"energy": seat + 1}),
    ):
        @pl.when(present)
        def _():
            pl.semaphore_signal(barrier, inc=1, device_id=target, device_id_type=MESH)

    eye = (
        lax.broadcasted_iota(jnp.int32, (width, width), 0)
        == lax.broadcasted_iota(jnp.int32, (width, width), 1)
    )
    for param in params[:3]:
        param.wait()
    hop = between[0]
    own = jnp.where(eye, onsite[0:1, :], 0.0) + 0.5 * (within[0] + within[0].T)
    hamil[0] = own
    given[0] = hop
    given[1] = own

    def give(index):
        return pltpu.make_async_remote_copy(
            src_ref=sigma.at[0, index], dst_ref=sigma.at[1, index],
            send_sem=send_x.at[index], recv_sem=recv_x.at[index],
            device_id={"section": place - 1}, device_id_type=MESH,
        )

    def give_shared():
        return pltpu.make_async_remote_copy(
            src_ref=given.at[core], dst_ref=given.at[2 + core],
            send_sem=send_g.at[0], recv_sem=recv_g.at[0],
            device_id={"section": place - 1}, device_id_type=MESH,
        )

    def give_partner():
        return pltpu.make_async_remote_copy(
            src_ref=given.at[2 + core], dst_ref=given.at[2 + core],
            send_sem=send_g.at[1], recv_sem=recv_g.at[1],
            device_id=partner, device_id_type=MESH,
        )

    def set_hops(which, value):
        hops[which, 0], hops[which, 1] = split(value)
        hops[which, 2], hops[which, 3] = split(value.T)

    set_hops(0, hop)

    @pl.when(seat == 0)
    def _():
        halo[0:REACH] = jnp.zeros((REACH, 2, width, width), F32)

    @pl.when(seat == spans - 1)
    def _():
        halo[REACH : 2 * REACH] = jnp.zeros((REACH, 2, width, width), F32)

    @pl.when(place == 0)
    def _():
        left[0] = jnp.zeros((width, width), F32)
        left[1] = -CONTACT * matmul((hops[0, 2], hops[0, 3]), (hops[0, 0], hops[0, 1]))

    def set_mats():
        for param in params[3:]:
            param.wait()
        row_group = jnp.broadcast_to(groups[0:1, :].astype(F32), (width, width))
        mat = jnp.where(row_group == row_group.T, coupling[0], 0.0)
        mats[0], mats[1] = split(mat)
        mats[2], mats[3] = split(mat.T)
        outer[...] = mats[...]

        @pl.when(has_prev)
        def _():
            outer[...] = hops[0]


    def inverse(index, which, left_re, left_im):
        number = jnp.full((1, width), 2 * (seat * count + index) + 1, jnp.int32)
        energy = -1.0 + number.astype(F32) / (count * spans)
        sys_re = jnp.where(eye, energy, 0.0) - hamil[which] - sigma[which, index, 0] - left_re
        sys_im = jnp.where(eye, ETA, 0.0) - sigma[which, index, 1] - left_im
        diag_re = jnp.where(eye, sys_re, 0.0)
        diag_im = jnp.where(eye, sys_im, 0.0)
        inverses = []
        for axis in (1, 0):
            real_c = jnp.sum(diag_re, axis=axis, keepdims=True)
            imag_c = jnp.sum(diag_im, axis=axis, keepdims=True)
            modulus = real_c * real_c + imag_c * imag_c
            inverses.append((real_c / modulus, -imag_c / modulus))
        (col_re, col_im), (row_re, row_im) = inverses
        rest_re = jnp.where(eye, 0.0, sys_im * row_im - sys_re * row_re)
        rest_im = jnp.where(eye, 0.0, -(sys_re * row_im + sys_im * row_re))
        square_re, square_im = complex_matmul((rest_re, rest_im), (rest_re, rest_im))
        powers_re, powers_im = complex_matmul(
            (jnp.concatenate([rest_re, square_re], 0), jnp.concatenate([rest_im, square_im], 0)),
            (square_re, square_im),
        )
        sum_re = jnp.where(eye, 1.0, 0.0) + rest_re + square_re + powers_re[:width]
        sum_im = rest_im + square_im + powers_im[:width]
        base_re = col_re * sum_re - col_im * sum_im
        base_im = col_re * sum_im + col_im * sum_re
        out_re, out_im = complex_matmul((base_re, base_im), (powers_re[width:], powers_im[width:]))
        return base_re + out_re, base_im + out_im

    def invert(index):
        local[0, index, 0], local[0, index, 1] = inverse(index, 0, left[0], left[1])

    if paced:
        @pl.when(pacing)
        def _():
            load(order(0)).wait()
            invert(order(0))

    peers = sum(present.astype(jnp.int32) for present in (has_prev, has_next, has_low, has_high))
    pl.semaphore_wait(barrier, peers)

    @pl.when(leaf & has_prev)
    def _():
        give_shared().start()
        for step in range(count):
            index = order(step)
            load(index).wait()
            give(index).start()

    @pl.when(has_prev)
    def _():
        set_mats()

    @pl.when(folding & has_next)
    def _():
        give_shared().wait_recv()
        give_partner().start()
        give_partner().wait_recv()
        set_hops(1, given[2])
        hamil[1] = given[3]

    def forward_copy(which, index, part):
        rows = pl.ds(edges[part], edges[part + 1] - edges[part])
        return pltpu.make_async_remote_copy(
            src_ref=local.at[which, index, :, rows], dst_ref=came_f.at[index, :, rows],
            send_sem=send_f.at[index, part], recv_sem=recv_f.at[index, part],
            device_id={"section": place + 1}, device_id_type=MESH,
        )

    def backward_copy(index, part):
        rows = pl.ds(edges[part], edges[part + 1] - edges[part])
        return pltpu.make_async_remote_copy(
            src_ref=sent_b.at[index, :, rows], dst_ref=came_b.at[index, :, rows],
            send_sem=send_b.at[index, part], recv_sem=recv_b.at[index, part],
            device_id={"section": place - 1}, device_id_type=MESH,
        )

    def halo_up(index):
        slot = index - (count - REACH)
        return pltpu.make_async_remote_copy(
            src_ref=field_y.at[index], dst_ref=halo.at[slot],
            send_sem=send_h.at[slot], recv_sem=recv_h.at[slot],
            device_id={"energy": seat + 1}, device_id_type=MESH,
        )

    def halo_down(index):
        slot = index + REACH
        return pltpu.make_async_remote_copy(
            src_ref=field_y.at[index], dst_ref=halo.at[slot],
            send_sem=send_h.at[slot], recv_sem=recv_h.at[slot],
            device_id={"energy": seat - 1}, device_id_type=MESH,
        )

    def contact(index):
        halves = []
        for part in range(CHUNKS):
            forward_copy(0, index, part).wait_recv()
            rows = slice(edges[part], edges[part + 1])
            field = [split(came_f[index, side, rows]) for side in range(2)]
            half = matmul(join(field, 0), (hops[0, 0], hops[0, 1]))
            size = edges[part + 1] - edges[part]
            halves.append(join([split(half[:size]), split(half[size:])], 1))
        result = matmul((hops[0, 2], hops[0, 3]), join(halves, 0))
        left[0], left[1] = result[:, :width], result[:, width:]

    def launch(index, which):
        for part in range(CHUNKS):
            forward_copy(which, index, part).start()

    def forward(step):
        ahead = step
        if paced:
            ahead = step + pacing.astype(jnp.int32)

            @pl.when(pacing)
            def _():
                @pl.when((step > 0) | odd)
                def _():
                    pl.semaphore_wait(turns, 1)

                launch(order(step), 0)

        @pl.when(ahead < count)
        def _():
            index = order(ahead)
            load(index).wait()

            @pl.when(has_prev)
            def _():
                contact(index)

            invert(index)

            @pl.when(jnp.logical_not(pacing) & (place < fold))
            def _():
                launch(index, 0)

        if paced:
            @pl.when(pacing & ((step < count - 1) | (core == 0)))
            def _():
                forward_copy(0, order(step), CHUNKS - 2).wait_send()
                pl.semaphore_signal(turns, inc=1, device_id=partner, device_id_type=MESH)

    def publish(index):
        return pltpu.make_async_copy(green.at[index], green_out.at[index], keep_g.at[index])

    def publish_total(index):
        return pltpu.make_async_copy(total.at[index], total_out.at[index], keep_t.at[index])

    def neighbours(index):
        @pl.when(has_high & (index >= count - REACH))
        def _():
            halo_up(index).start()

        @pl.when(has_low & (index < REACH))
        def _():
            halo_down(index).start()

    def finish(index):
        field = join([split(green[index, 0, side]) for side in range(2)], 0)
        half = matmul(field, (mats[2], mats[3]))
        half = join([split(half[:width]), split(half[width:])], 1)
        result = matmul((mats[0], mats[1]), half)
        field_y[index, 0] = result[:, :width]
        field_y[index, 1] = result[:, width:]
        neighbours(index)

    def send_back(index, out_re, out_im):
        sent_b[index, 0] = out_re
        sent_b[index, 1] = out_im
        for part in range(CHUNKS):
            backward_copy(index, part).start()

    def prepare(index):
        base = [split(local[0, index, side]) for side in range(2)]
        lefts = matmul((outer[0], outer[1]), join(base, 1))
        rights = matmul(join(base, 0), (outer[2], outer[3]))
        lefts = splits(lefts[:, :width], lefts[:, width:])
        ready_r[0], ready_r[1] = complex_columns(splits(rights[:width], rights[width:]))
        ready_w[...] = matmul(join(lefts, 0), (outer[2], outer[3]))
        ready_l[0], ready_l[1] = complex_rows(lefts)

    def backward(index):
        columns = ready_r[0], ready_r[1]
        mids = []
        for part in range(CHUNKS):
            backward_copy(index, part).wait_recv()
            rows = slice(edges[part], edges[part + 1])
            incoming = join([split(came_b[index, side, rows]) for side in range(2)], 1)
            mids.append(matmul(incoming, columns))
        mid = jnp.concatenate(mids, axis=0)
        out = matmul((ready_l[0], ready_l[1]), complex_columns(splits(mid[:, :width], mid[:, width:])))
        out_re, out_im = ready_w[:width] + out[:, :width], ready_w[width:] + out[:, width:]

        @pl.when(has_prev)
        def _():
            send_back(index, out_re, out_im)

        @pl.when(jnp.logical_not(has_prev))
        def _():
            field_y[index, 0] = out_re
            field_y[index, 1] = out_im
            neighbours(index)

        base_re, base_im = local[0, index, 0], local[0, index, 1]
        mid = complex_matmul((came_b[index, 0], came_b[index, 1]), (base_re, base_im))
        out_re, out_im = complex_matmul((base_re, base_im), mid)
        green[index, 0, 0] = base_re + out_re
        green[index, 0, 1] = base_im + out_im
        publish(index).start()

        @pl.when(has_prev)
        def _():
            finish(index)

    def refold(index):
        give(index).wait_recv()
        base_re, base_im = local[0, index, 0], local[0, index, 1]
        base = splits(base_re, base_im)
        half = matmul(join(base, 0), (hops[1, 0], hops[1, 1]))
        half_re, half_im = half[:width], half[width:]
        half = join(splits(half_re, half_im), 1)
        result = matmul((hops[1, 2], hops[1, 3]), half)
        end_re, end_im = inverse(index, 1, result[:, :width], result[:, width:])
        outer_l = matmul((hops[0, 0], hops[0, 1]), half)
        inner_r = matmul((hops[1, 2], hops[1, 3]), join(base, 1))
        inner_re, inner_im = inner_r[:, :width], inner_r[:, width:]
        outer_r = matmul(join(splits(inner_re, inner_im), 0), (hops[0, 2], hops[0, 3]))
        whole = matmul((hops[0, 0], hops[0, 1]), join(base, 1))
        whole = join(splits(whole[:, :width], whole[:, width:]), 0)
        whole = matmul(whole, (hops[0, 2], hops[0, 3]))
        mid = complex_matmul((end_re, end_im), (outer_r[:width], outer_r[width:]))
        out_re, out_im = complex_matmul((outer_l[:, :width], outer_l[:, width:]), mid)
        local[1, index, 0], local[1, index, 1] = end_re, end_im

        @pl.when(has_prev)
        def _():
            send_back(index, whole[:width] + out_re, whole[width:] + out_im)

        launch(index, 1)
        mid = complex_matmul((local[1, index, 0], local[1, index, 1]), (inner_re, inner_im))
        out_re, out_im = complex_matmul((half_re, half_im), mid)
        green[index, 0, 0] = local[0, index, 0] + out_re
        green[index, 0, 1] = local[0, index, 1] + out_im
        publish(index).start()
        finish(index)

    def receive(index):
        for part in range(CHUNKS):
            forward_copy(0, index, part).wait_recv()
        green[index, 0] = came_f[index]
        publish(index).start()
        finish(index)

    behind = 2 * (fold - place)

    def turn(step, carry):
        @pl.when((place <= fold) & (step < count))
        def _():
            forward(step)

        @pl.when((step == 0) & jnp.logical_not(has_prev))
        def _():
            set_mats()

        @pl.when((place < fold) & (step >= behind) & (step < behind + count))
        def _():
            backward(order(step - behind))

        @pl.when((place < fold) & (step + 1 >= behind) & (step + 1 < behind + count))
        def _():
            prepare(order(step + 1 - behind))

        @pl.when(folding & has_next & (step < count))
        def _():
            refold(order(step))

        @pl.when(leaf & has_prev & (step < count))
        def _():
            receive(order(step))

        return carry

    lax.fori_loop(0, count + 2 * fold, turn, 0)

    near = jnp.float32(0.0)
    far = jnp.float32(0.0)
    for mode in range(offsets.shape[0]):
        near = near + jnp.where(offsets[mode] == 1, strength[mode], 0.0)
        far = far + jnp.where(offsets[mode] == 2, strength[mode], 0.0)

    def block(index, side):
        if index < 0:
            return halo[index + REACH, side]
        if index >= count:
            return halo[index - count + REACH, side]
        return field_y[index, side]

    @pl.when(has_low)
    def _():
        for slot in range(REACH):
            halo_up(count - REACH + slot).wait_recv()

    for index in range(count):
        if index == max(count - REACH, 0):
            @pl.when(has_high)
            def _():
                for slot in range(REACH):
                    halo_down(slot).wait_recv()

        for side in range(2):
            total[index, 0, side] = near * (
                block(index - 1, side) + block(index + 1, side)
            ) + far * (block(index - 2, side) + block(index + 2, side))
        publish_total(index).start()

    @pl.when(has_next)
    def _():
        for step in range(count):
            for part in range(CHUNKS):
                if paced and part == CHUNKS - 2:
                    waited = pacing & ((step < count - 1) | (core == 0))

                    @pl.when(jnp.logical_not(waited))
                    def _():
                        forward_copy(0, order(step), part).wait_send()
                else:
                    forward_copy(0, order(step), part).wait_send()

    @pl.when(has_prev & (place < last))
    def _():
        for index in range(count):
            for part in range(CHUNKS):
                backward_copy(index, part).wait_send()

    @pl.when(leaf & has_prev)
    def _():
        give_shared().wait_send()
        for index in range(count):
            give(index).wait_send()

    @pl.when(folding & has_next)
    def _():
        give_partner().wait_send()

    @pl.when(has_high)
    def _():
        for slot in range(REACH):
            halo_up(count - REACH + slot).wait_send()

    @pl.when(has_low)
    def _():
        for slot in range(REACH):
            halo_down(slot).wait_send()

    for index in range(count):
        publish(index).wait()
        publish_total(index).wait()


def deliver(green, total, green_out, self_out, held, load, save):
    count = green.shape[0]
    loads, saves = [], []
    for side, (source, target) in enumerate(((green, green_out), (total, self_out))):
        for index in range(count):
            slot = side * count + index
            for part in range(2):
                here, way = (slot, 0, part), (index, 0, part)
                loads.append(pltpu.make_async_copy(source.at[way], held.at[here], load.at[slot, part]))
                saves.append(pltpu.make_async_copy(held.at[here], target.at[way], save.at[slot, part]))
    for copy in loads:
        copy.start()
    for arrival, departure in zip(loads, saves):
        arrival.wait()
        departure.start()
    for copy in saves:
        copy.wait()


def per_device(self_in, onsite, within, between, coupling, groups, offsets, strength):
    count, width = self_in.shape[0], self_in.shape[3]
    smem = pl.BlockSpec(memory_space=pltpu.SMEM)
    hbm = pl.BlockSpec(memory_space=pltpu.HBM)
    shape = jax.ShapeDtypeStruct(self_in.shape, F32)
    dma = pltpu.SemaphoreType.DMA
    blocks = pltpu.VMEM((count, 2, width, width), F32)
    green, total = pl.pallas_call(
        kernel,
        out_shape=(shape, shape),
        in_specs=[smem] * 2 + [hbm] * 6,
        out_specs=(hbm, hbm),
        scratch_shapes=[
            pltpu.VMEM(self_in.shape, F32),
            pltpu.VMEM(self_in.shape, F32),
            dma((count,)), dma((count,)),
            pltpu.VMEM(onsite.shape, F32),
            pltpu.VMEM(within.shape, F32),
            pltpu.VMEM(between.shape, F32),
            pltpu.VMEM(coupling.shape, F32),
            pltpu.VMEM(groups.shape, jnp.int32),
            dma((5,)),
            pltpu.VMEM((2, width, 2 * width), BF16),
            pltpu.VMEM((2, 2 * width, 2 * width), BF16),
            pltpu.VMEM((2 * width, width), F32),
            pltpu.VMEM((2, width, width), F32),
            pltpu.VMEM((2, 4, width, width), BF16),
            pltpu.VMEM((4, width, width), BF16),
            pltpu.VMEM((4, width, width), BF16),
            pltpu.VMEM((2, width, width), F32),
            pltpu.VMEM((2, count, 2, width, width), F32),
            pltpu.VMEM((2, count, 2, width, width), F32),
            blocks, blocks, blocks,
            pltpu.VMEM((4, width, width), F32),
            blocks,
            pltpu.VMEM((2 * REACH, 2, width, width), F32),
            dma((count,)),
            dma((count, CHUNKS)), dma((count, CHUNKS)), dma((count, CHUNKS)), dma((count, CHUNKS)),
            dma((2 * REACH,)), dma((2 * REACH,)),
            dma((count,)), dma((count,)), dma((2,)), dma((2,)),
            pltpu.SemaphoreType.REGULAR,
        ],
        compiler_params=pltpu.CompilerParams(
            collective_id=0, has_side_effects=True, vmem_limit_bytes=60 * 2**20
        ),
    )(offsets, strength, self_in, onsite, within, between, coupling, groups)
    return pl.pallas_call(
        deliver,
        out_shape=(shape, shape),
        in_specs=[hbm] * 2,
        out_specs=(hbm, hbm),
        scratch_shapes=[
            pltpu.VMEM((2 * count,) + self_in.shape[1:], F32),
            dma((2 * count, 2)), dma((2 * count, 2)),
        ],
        compiler_params=pltpu.CompilerParams(vmem_limit_bytes=60 * 2**20),
    )(green, total)


def solution(mesh):
    placed = (
        P("energy", "section", None, None, None),
        P("section", None),
        P("section", None, None),
        P("section", None, None),
        P("section", None, None),
        P("section", None),
        P(),
        P(),
    )
    return jax.shard_map(
        per_device,
        mesh=mesh,
        in_specs=placed,
        out_specs=(
            P("energy", "section", None, None, None),
            P("energy", "section", None, None, None),
        ),
        check_vma=False,
    )
```
